256 devices in a mesh: dp: 8 (over z_lo, x), ctx: 32 (over z_hi, y, core).
Axes of the slice: x: 4, y: 4, z: 8 (z_hi: 4, z_lo: 2; z = z_hi * 2 + z_lo), core: 2. Of those that a mesh axis runs over, the one named last changes fastest.
Arguments:
- queries: bfloat16 [8, 4096, 2048], P('dp', 'ctx'), may hold values from -6 to 6
- keys: bfloat16 [8, 4096, 2048], P('dp', 'ctx'), may hold values from -6 to 6
- values: bfloat16 [8, 4096, 2048], P('dp', 'ctx'), may hold values from -6 to 6
- upstream: bfloat16 [8, 4096, 2048], P('dp', 'ctx'), may hold values from -6 to 6
- filters: float32 [2048, 4096], P('ctx'), may hold values from -0.09375 to 0.09375
- out_weight: bfloat16 [2048, 2048], P('ctx'), may hold values from -0.125 to 0.125
Outputs:
- grad_queries: bfloat16 [8, 4096, 2048], P('dp', 'ctx')
- grad_keys: bfloat16 [8, 4096, 2048], P('dp', 'ctx')
- grad_values: bfloat16 [8, 4096, 2048], P('dp', 'ctx')
- grad_filters: float32 [2048, 4096], P('ctx')
- grad_weight: float32 [2048, 2048], P('ctx')
The draws below stay inside these ranges and needn't reach their ends.
All inputs are finite; a program needn't handle non-finite values.
Results may differ from the reference program's by a relative error of at most 0.019.
Values may be sent and summed in bfloat16 or wider, within the bound.
A program may use at most 128 MiB of HBM per device.

```python
import jax
import jax.numpy as jnp
from jax import lax

C = 2048
D = 2048
SEQS = 8
SEQ_LEN = 4096


def steps_of(rng, shape, pieces, low, high):
    def one(position, parts):
        draws = jax.random.uniform(jax.random.fold_in(jax.random.fold_in(rng, 6), position), (parts,), jnp.float32, low / len(pieces), high / len(pieces))
        return jnp.repeat(jnp.exp(draws), shape[position] // parts).reshape((-1,) + (1,) * (len(shape) - position - 1))

    factor_of = one(*pieces[0])
    for cut in pieces[1:]:
        factor_of = factor_of * one(*cut)
    return factor_of


def bell_draw(key, shape, width, reach, shards=(), dtype=jnp.bfloat16):
    array = jax.random.normal(key, shape, jnp.float32) * width
    if len(shards) > 0:
        array = steps_of(key, shape, shards, -0.22, 0.18) * array
    return jnp.clip(array, min=-reach, max=reach).astype(dtype)


def setup_inputs(seed: int = 0) -> dict:
    arg_keys = jax.random.split(jax.random.key(seed), 7)
    return {
        "queries": bell_draw(arg_keys[0], (SEQS, SEQ_LEN, C), 1.0, 6.0, ((0, 8), (1, 32))),
        "keys": bell_draw(arg_keys[1], (SEQS, SEQ_LEN, C), 1.0, 6.0, ((0, 8), (1, 32))),
        "values": bell_draw(arg_keys[2], (SEQS, SEQ_LEN, C), 1.0, 6.0, ((0, 8), (1, 32))),
        "upstream": bell_draw(arg_keys[3], (SEQS, SEQ_LEN, D), 1.0, 6.0, ((0, 8), (1, 32))),
        "filters": bell_draw(arg_keys[4], (C, SEQ_LEN), SEQ_LEN ** -0.5, 0.09375, ((0, 32),), jnp.float32),
        "out_weight": bell_draw(arg_keys[5], (C, D), D ** -0.5, 0.125, ((0, 32),)),
    }


def reference(queries, keys, values, upstream, filters, out_weight):
    fft_len = 2 * SEQ_LEN
    upstream_rows = upstream.reshape(SEQS * SEQ_LEN, D)
    grad_gated = jnp.dot(upstream_rows, out_weight.T, preferred_element_type=jnp.float32).astype(jnp.bfloat16)
    grad_gated = grad_gated.reshape(SEQS, SEQ_LEN, C)
    mixed_rows = (keys.astype(jnp.float32) * values.astype(jnp.float32)).astype(jnp.bfloat16)
    scaled = (grad_gated.astype(jnp.float32) * queries.astype(jnp.float32)).astype(jnp.bfloat16)
    filter_spec = jnp.fft.rfft(filters.astype(jnp.float32).T, n=fft_len, axis=0)

    def per_sequence(running, inputs):
        mixed_seq, scaled_seq = inputs
        mix_spec = jnp.fft.rfft(mixed_seq.astype(jnp.float32), n=fft_len, axis=0)
        grad_spec = jnp.fft.rfft(scaled_seq.astype(jnp.float32), n=fft_len, axis=0)
        conv_out = jnp.fft.irfft(filter_spec * mix_spec, n=fft_len, axis=0)[:SEQ_LEN]
        back_grad = jnp.fft.irfft(jnp.conj(filter_spec) * grad_spec, n=fft_len, axis=0)[:SEQ_LEN]
        filter_part = jnp.fft.irfft(jnp.conj(mix_spec) * grad_spec, n=fft_len, axis=0)[:SEQ_LEN]
        return running + filter_part.astype(jnp.float32), (conv_out.astype(jnp.bfloat16), back_grad.astype(jnp.bfloat16))

    grad_filters, outputs = lax.scan(per_sequence, jnp.zeros((SEQ_LEN, C), jnp.float32), (mixed_rows, scaled))
    conv_out, back_grad = outputs
    conv_wide = conv_out.astype(jnp.float32)
    back_wide = back_grad.astype(jnp.float32)
    grad_queries = (grad_gated.astype(jnp.float32) * conv_wide).astype(jnp.bfloat16)
    grad_keys = (back_wide * values.astype(jnp.float32)).astype(jnp.bfloat16)
    grad_values = (back_wide * keys.astype(jnp.float32)).astype(jnp.bfloat16)
    gated_rows = (queries.astype(jnp.float32) * conv_wide).astype(jnp.bfloat16).reshape(SEQS * SEQ_LEN, C)
    grad_weight = jnp.dot(gated_rows.T, upstream_rows, preferred_element_type=jnp.float32)
    return grad_queries, grad_keys, grad_values, grad_filters.T, grad_weight
```

```python
import functools
import math

import jax
import jax.numpy as jnp
import numpy as np
from jax import lax
from jax.experimental import pallas as pl
from jax.experimental.pallas import tpu as pltpu
from jax.sharding import PartitionSpec as P

NX, NZL, NZH, NY, NC = 4, 2, 4, 4, 2
TOK, CH = 128, 64
BF, F32 = jnp.bfloat16, jnp.float32
MESH = pl.DeviceIdType.MESH


def place():
    dp = lax.axis_index("dp")
    ctx = lax.axis_index("ctx")
    near = NY * NC
    return dict(
        dp=dp,
        ctx=ctx,
        x=lax.rem(dp, NX),
        zl=dp // NX,
        zh=ctx // near,
        near=lax.rem(ctx, near),
        y=lax.rem(ctx, near) // NC,
        core=lax.rem(ctx, NC),
    )


def send(src, dst, ssem, rsem, dp, ctx):
    return pltpu.make_async_remote_copy(
        src_ref=src,
        dst_ref=dst,
        send_sem=ssem,
        recv_sem=rsem,
        device_id=(dp, ctx),
        device_id_type=MESH,
    )


def greet(peers):
    barrier = pltpu.get_barrier_semaphore()
    for dp, ctx in peers:
        pl.semaphore_signal(barrier, inc=1, device_id=(dp, ctx), device_id_type=MESH)
    pl.semaphore_wait(barrier, len(peers))


def gather_kernel(
    mix_ref, query_ref, up_ref, w_ref,
    mixed_out, scaled_out, gg_out, query_out, up_out,
    up_all, w_all, q_all, gg_all, sc_all,
    up_send, up_recv, w_send, w_recv, q_send, q_recv, m_send, m_recv, s_send, s_recv, local,
):
    at = place()
    dp, ctx, near, zh, y, core = (at[k] for k in ("dp", "ctx", "near", "zh", "y", "core"))
    nctx, nnear = NZH * NY * NC, NY * NC
    greet([(dp, lax.rem(ctx + s, nctx)) for s in range(1, nctx)])

    own_w = pltpu.make_async_copy(w_ref, w_all.at[zh], local.at[0])
    own_u = pltpu.make_async_copy(up_ref, up_all.at[near], local.at[1])
    own_q = pltpu.make_async_copy(query_ref.at[:, near], q_all.at[near], local.at[2])
    own_m = pltpu.make_async_copy(mix_ref.at[ctx], mixed_out.at[ctx], local.at[3])
    for copy in (own_w, own_u, own_q, own_m):
        copy.start()

    partner = zh * nnear + y * NC + lax.rem(core + 1, NC)
    ups = {}
    order = [2, 1, 3] if NY == 4 else list(range(1, NY))
    for dy in order:
        there = zh * nnear + lax.rem(y + dy, NY) * NC + core
        ups[dy] = send(up_ref, up_all.at[near], up_send.at[dy], up_recv.at[dy], dp, there)
        ups[dy].start()
    pair = send(up_ref, up_all.at[near], up_send.at[0], up_recv.at[0], dp, partner)
    pair.start()
    ws = []
    for s in range(1, NZH):
        there = lax.rem(zh + s, NZH) * nnear + near
        ws.append(send(w_ref, w_all.at[zh], w_send.at[s], w_recv.at[s], dp, there))
        ws[-1].start()
    qs = []
    for s in range(1, nnear):
        to = lax.rem(near + s, nnear)
        qs.append(
            send(query_ref.at[:, to], q_all.at[near], q_send.at[s], q_recv.at[s], dp, zh * nnear + to)
        )
        qs[-1].start()
    ms = []
    for s in range(1, nctx):
        to = lax.rem(ctx + s, nctx)
        ms.append(send(mix_ref.at[to], mixed_out.at[ctx], m_send.at[s], m_recv.at[s], dp, to))
        ms[-1].start()

    for copy in (own_w, own_u, own_q):
        copy.wait()
    relays = {}
    outs = []
    sent = []

    def keep(slot, k):
        copy = pltpu.make_async_copy(up_all.at[slot], up_out.at[slot], local.at[8 + k])
        copy.start()
        outs.append(copy)

    def work(slot, k):
        up = up_all[slot]
        w = w_all[...].reshape(NZH * CH, up.shape[-1])
        gg = lax.dot_general(w, up, (((1,), (1,)), ((), ())), preferred_element_type=F32).astype(BF)
        gg = gg.reshape(NZH, CH, TOK)
        gg_all[slot] = gg
        sc_all[slot] = (gg.astype(F32) * q_all[slot].astype(F32)).astype(BF)
        n = zh * nnear + slot
        mine = pltpu.make_async_copy(sc_all.at[slot, zh], scaled_out.at[n], local.at[16 + k])
        mine.start()
        outs.append(mine)
        for s in range(1, NZH):
            to = lax.rem(zh + s, NZH)
            copy = send(
                sc_all.at[slot, to], scaled_out.at[n],
                s_send.at[k, s], s_recv.at[k, s], dp, to * nnear + near,
            )
            copy.start()
            sent.append(copy)

    for copy in ws + qs:
        copy.wait_recv()
    keep(near, 0)
    work(near, 0)
    far = []
    for i, dy in enumerate([1, 3, 2] if NY == 4 else list(range(1, NY))):
        slot = lax.rem(y + NY - dy, NY) * NC + core
        ups[dy].wait_recv()
        relays[dy] = send(
            up_all.at[slot], up_all.at[slot],
            up_send.at[NY + dy], up_recv.at[NY + dy], dp, partner,
        )
        relays[dy].start()
        keep(slot, 1 + i)
        work(slot, 1 + i)
        far.append((dy, lax.rem(y + NY - dy, NY) * NC + lax.rem(core + 1, NC)))
    pair.wait_recv()
    slot = y * NC + lax.rem(core + 1, NC)
    keep(slot, NY)
    work(slot, NY)
    for i, (dy, slot) in enumerate(far):
        relays[dy].wait_recv()
        keep(slot, NY + 1 + i)
        work(slot, NY + 1 + i)
    last = [
        pltpu.make_async_copy(gg_all, gg_out, local.at[4]),
        pltpu.make_async_copy(q_all, query_out, local.at[5]),
    ]
    for copy in last:
        copy.start()
    for copy in outs + last + [own_m]:
        copy.wait()
    for copy in list(ups.values()) + [pair] + ws + qs + list(relays.values()):
        copy.wait_send()
    for copy in ms + sent:
        copy.wait()


def gather_call(mix, query, up, w):
    nctx, nnear = NZH * NY * NC, NY * NC
    depth = up.shape[-1]
    dma = pltpu.SemaphoreType.DMA
    hbm = pl.BlockSpec(memory_space=pl.ANY)
    vmem = pl.BlockSpec(memory_space=pltpu.VMEM)
    return pl.pallas_call(
        gather_kernel,
        name="gather",
        out_shape=[
            jax.ShapeDtypeStruct((nctx, CH, TOK), BF),
            jax.ShapeDtypeStruct((nctx, CH, TOK), BF),
            jax.ShapeDtypeStruct((nnear, NZH, CH, TOK), BF),
            jax.ShapeDtypeStruct((nnear, NZH, CH, TOK), BF),
            jax.ShapeDtypeStruct((nnear, TOK, depth), BF),
        ],
        in_specs=[vmem] * 4,
        out_specs=[hbm] * 5,
        scratch_shapes=[
            pltpu.VMEM((nnear, TOK, depth), BF),
            pltpu.VMEM((NZH, CH, depth), BF),
            pltpu.VMEM((nnear, NZH, CH, TOK), BF),
            pltpu.VMEM((nnear, NZH, CH, TOK), BF),
            pltpu.VMEM((nnear, NZH, CH, TOK), BF),
            dma((2 * NY,)), dma((2 * NY,)),
            dma((NZH,)), dma((NZH,)),
            dma((nnear,)), dma((nnear,)),
            dma((nctx,)), dma((nctx,)),
            dma((nnear, NZH)), dma((nnear, NZH)),
            dma((24,)),
        ],
        compiler_params=pltpu.CompilerParams(
            collective_id=0, has_side_effects=True, vmem_limit_bytes=40 << 20
        ),
    )(mix, query, up, w)


def scatter_kernel(
    conv_ref, back_ref, fg_ref, gg_ref, query_ref, up_ref,
    gq_out, back_out, fg_out, gw_out,
    conv_all, gg_all, q_all, up_all, gate, gq_all,
    fg_x, fg_half, fg_z, fg_fin, gw_part, gw_x, gw_mid, gw_z, gw_fin,
    c_send, c_recv, b_send, b_recv, fx_send, fx_recv, fz_send, fz_recv, fa_send, fa_recv,
    g_send, g_recv, wx_send, wx_recv, wz_send, wz_recv, wa_send, wa_recv, local,
):
    at = place()
    dp, ctx, near, zh, zl, x = (at[k] for k in ("dp", "ctx", "near", "zh", "zl", "x"))
    nctx, nnear, ndp, nz = NZH * NY * NC, NY * NC, NX * NZL, NZH * NZL
    rows = CH // NX
    span = fg_ref.shape[1] // NZL
    depth = up_ref.shape[-1]
    wide, narrow = depth // NX, depth // NX // NZL
    peers = [(dp, lax.rem(ctx + s, nctx)) for s in range(1, nctx)]
    peers += [(lax.rem(dp + s, ndp), ctx) for s in range(1, ndp)]
    other = lax.rem(zl + 1, NZL) * NX + x
    if NZL > 1:
        peers += [(other, lax.rem(zh + s, NZH) * nnear + near) for s in range(1, NZH)]

    loads = [
        pltpu.make_async_copy(gg_ref, gg_all, local.at[0]),
        pltpu.make_async_copy(query_ref, q_all, local.at[1]),
        pltpu.make_async_copy(up_ref, up_all, local.at[2]),
        pltpu.make_async_copy(conv_ref.at[pl.ds(zh * nnear, nnear)], conv_all.at[zh], local.at[3]),
        pltpu.make_async_copy(fg_ref.at[pl.ds(x * rows, rows)], fg_x.at[x], local.at[4]),
    ]
    for copy in loads:
        copy.start()
    own_b = pltpu.make_async_copy(back_ref.at[ctx], back_out.at[ctx], local.at[5])
    own_b.start()
    greet(peers)

    cs = []
    for s in range(1, NZH):
        to = lax.rem(zh + s, NZH)
        cs.append(
            send(
                conv_ref.at[pl.ds(to * nnear, nnear)], conv_all.at[zh],
                c_send.at[s], c_recv.at[s], dp, to * nnear + near,
            )
        )
        cs[-1].start()
    fxs = []
    for s in range(1, NX):
        to = lax.rem(x + s, NX)
        fxs.append(
            send(
                fg_ref.at[pl.ds(to * rows, rows)], fg_x.at[x],
                fx_send.at[s], fx_recv.at[s], zl * NX + to, ctx,
            )
        )
        fxs[-1].start()
    bs = []
    for s in range(1, nctx):
        to = lax.rem(ctx + s, nctx)
        bs.append(send(back_ref.at[to], back_out.at[ctx], b_send.at[s], b_recv.at[s], dp, to))
        bs[-1].start()
    for copy in loads:
        copy.wait()

    for copy in fxs:
        copy.wait_recv()
    total = fg_x[0].astype(F32)
    for i in range(1, NX):
        total = total + fg_x[i].astype(F32)
    for i in range(NZL):
        fg_half[i] = total[:, i * span : (i + 1) * span].astype(BF)
    fzs = []
    for s in range(1, NZL):
        to = lax.rem(zl + s, NZL)
        fzs.append(
            send(fg_half.at[to], fg_z.at[zl], fz_send.at[s], fz_recv.at[s], to * NX + x, ctx)
        )
        fzs[-1].start()
    own_f = pltpu.make_async_copy(fg_half.at[zl], fg_z.at[zl], local.at[6])
    own_f.start()

    for copy in cs:
        copy.wait_recv()
    for i in range(nnear):
        for h in range(NZH):
            conv = conv_all[h, i].astype(F32)
            gq_all[i, h] = (gg_all[i, h].astype(F32) * conv).astype(BF)
            gate[h * CH : (h + 1) * CH, i * TOK : (i + 1) * TOK] = (
                q_all[i, h].astype(F32) * conv
            ).astype(BF)
    gs = []
    for s in range(1, nnear):
        to = lax.rem(near + s, nnear)
        gs.append(
            send(gq_all.at[to], gq_out.at[:, near], g_send.at[s], g_recv.at[s], dp, zh * nnear + to)
        )
        gs[-1].start()
    own_g = pltpu.make_async_copy(gq_all.at[near], gq_out.at[:, near], local.at[7])
    own_g.start()

    wxs = []
    for s in list(range(1, NX)) + [0]:
        to = lax.rem(x + s, NX)
        cols = pl.ds(pl.multiple_of(to * wide, wide), wide)
        up = up_all[:, :, cols].reshape(nnear * TOK, wide)
        gw_part[to] = jnp.dot(gate[...], up, preferred_element_type=F32).astype(BF)
        if s:
            wxs.append(
                send(gw_part.at[to], gw_x.at[x], wx_send.at[s], wx_recv.at[s], zl * NX + to, ctx)
            )
            wxs[-1].start()
    own_w = pltpu.make_async_copy(gw_part.at[x], gw_x.at[x], local.at[8])
    own_w.start()

    own_f.wait()
    for copy in fzs:
        copy.wait_recv()
    total = fg_z[0].astype(F32)
    for i in range(1, NZL):
        total = total + fg_z[i].astype(F32)
    fg_fin[...] = total.astype(BF)
    fas = []
    fslot = fg_out.at[pl.ds(x * rows, rows), pl.ds(pl.multiple_of(zl * span, span), span)]
    for s in range(1, ndp):
        to = lax.rem(dp + s, ndp)
        fas.append(send(fg_fin, fslot, fa_send.at[s], fa_recv.at[s], to, ctx))
        fas[-1].start()
    own_fa = pltpu.make_async_copy(fg_fin, fslot, local.at[9])
    own_fa.start()

    own_w.wait()
    for copy in wxs:
        copy.wait_recv()
    for h in range(NZH):
        total = gw_x[0, h * CH : (h + 1) * CH].astype(F32)
        for i in range(1, NX):
            total = total + gw_x[i, h * CH : (h + 1) * CH].astype(F32)
        for i in range(NZL):
            gw_mid[h, i] = total[:, i * narrow : (i + 1) * narrow].astype(BF)
    wzs = []
    k = 0
    for s in range(NZH):
        for l in range(NZL):
            if s or l:
                to, tl = lax.rem(zh + s, NZH), lax.rem(zl + l, NZL)
                wzs.append(
                    send(
                        gw_mid.at[to, tl], gw_z.at[zh * NZL + zl],
                        wz_send.at[k], wz_recv.at[k], tl * NX + x, to * nnear + near,
                    )
                )
                wzs[-1].start()
                k += 1
    own_z = pltpu.make_async_copy(gw_mid.at[zh, zl], gw_z.at[zh * NZL + zl], local.at[10])
    own_z.start()
    own_z.wait()
    for copy in wzs:
        copy.wait_recv()
    total = gw_z[0].astype(F32)
    for i in range(1, nz):
        total = total + gw_z[i].astype(F32)
    gw_fin[...] = total.astype(BF)
    was = []
    wslot = gw_out.at[:, pl.ds(pl.multiple_of((x * NZL + zl) * narrow, narrow), narrow)]
    for s in range(1, ndp):
        to = lax.rem(dp + s, ndp)
        was.append(send(gw_fin, wslot, wa_send.at[s], wa_recv.at[s], to, ctx))
        was[-1].start()
    own_wa = pltpu.make_async_copy(gw_fin, wslot, local.at[11])
    own_wa.start()

    for copy in (own_b, own_g, own_fa, own_wa):
        copy.wait()
    for copy in cs + fxs + fzs + wxs + wzs:
        copy.wait_send()
    for copy in bs + gs + fas + was:
        copy.wait()


def scatter_call(conv, back, fg, gg, query, up):
    nctx, nnear, ndp, nz = NZH * NY * NC, NY * NC, NX * NZL, NZH * NZL
    depth = up.shape[-1]
    seq = fg.shape[1]
    wide, narrow = depth // NX, depth // NX // NZL
    rows, span = CH // NX, seq // NZL
    dma = pltpu.SemaphoreType.DMA
    hbm = pl.BlockSpec(memory_space=pl.ANY)
    pairs = [NZH, nctx, NX, NZL, ndp, nnear, NX, nz, ndp]
    sems = [dma((n,)) for n in pairs for _ in range(2)]
    return pl.pallas_call(
        scatter_kernel,
        name="scatter",
        out_shape=[
            jax.ShapeDtypeStruct((NZH, nnear, CH, TOK), BF),
            jax.ShapeDtypeStruct((nctx, CH, TOK), BF),
            jax.ShapeDtypeStruct((CH, seq), BF),
            jax.ShapeDtypeStruct((CH, depth), BF),
        ],
        in_specs=[hbm] * 6,
        out_specs=[hbm] * 4,
        scratch_shapes=[
            pltpu.VMEM((NZH, nnear, CH, TOK), BF),
            pltpu.VMEM((nnear, NZH, CH, TOK), BF),
            pltpu.VMEM((nnear, NZH, CH, TOK), BF),
            pltpu.VMEM((nnear, TOK, depth), BF),
            pltpu.VMEM((NZH * CH, nnear * TOK), BF),
            pltpu.VMEM((nnear, NZH, CH, TOK), BF),
            pltpu.VMEM((NX, rows, seq), BF),
            pltpu.VMEM((NZL, rows, span), BF),
            pltpu.VMEM((NZL, rows, span), BF),
            pltpu.VMEM((rows, span), BF),
            pltpu.VMEM((NX, NZH * CH, wide), BF),
            pltpu.VMEM((NX, NZH * CH, wide), BF),
            pltpu.VMEM((NZH, NZL, CH, narrow), BF),
            pltpu.VMEM((nz, CH, narrow), BF),
            pltpu.VMEM((CH, narrow), BF),
        ]
        + sems
        + [dma((12,))],
        compiler_params=pltpu.CompilerParams(
            collective_id=1, has_side_effects=True, vmem_limit_bytes=40 << 20
        ),
    )(conv, back, fg, gg, query, up)


R2 = math.sqrt(0.5)


def add(a, b):
    return tuple(p if q is None else q if p is None else p + q for p, q in zip(a, b))


def neg(a):
    return tuple(None if p is None else -p for p in a)


def sub(a, b):
    return tuple(
        p if q is None else -q if p is None else p - q for p, q in zip(a, b)
    )


def conj(a):
    return (a[0], None if a[1] is None else -a[1])


def turn(a):
    return (None if a[1] is None else -a[1], a[0])


def unturn(a):
    return (a[1], None if a[0] is None else -a[0])


def times(a, angle):
    c, s = math.cos(angle), math.sin(angle)
    if a[1] is None:
        return (a[0] * c, a[0] * s)
    return (a[0] * c - a[1] * s, a[0] * s + a[1] * c)


def fft4(a, b, c, d, sign):
    s0, s1, s2, s3 = add(a, c), sub(a, c), add(b, d), sub(b, d)
    t3 = turn(s3) if sign > 0 else unturn(s3)
    return [add(s0, s2), add(s1, t3), sub(s0, s2), sub(s1, t3)]


def eighth(a, sign):
    if a[1] is None:
        return (a[0] * R2, a[0] * (R2 * sign))
    if sign > 0:
        return ((a[0] - a[1]) * R2, (a[0] + a[1]) * R2)
    return ((a[0] + a[1]) * R2, (a[1] - a[0]) * R2)


def fft8(v, sign):
    even = fft4(v[0], v[2], v[4], v[6], sign)
    odd = fft4(v[1], v[3], v[5], v[7], sign)
    quarter = turn if sign > 0 else unturn
    odd = [odd[0], eighth(odd[1], sign), quarter(odd[2]), quarter(eighth(odd[3], sign))]
    return [add(e, o) for e, o in zip(even, odd)] + [sub(e, o) for e, o in zip(even, odd)]


def split_rows(x):
    a = [[None] * 8 for _ in range(5)]
    for j in range(8):
        x0, x1, x2, x3 = x[j], x[8 + j], x[16 + j], x[24 + j]
        d, e = (x1 - x3) * R2, (x1 + x3) * R2
        s02, s13 = x0 + x2, x1 + x3
        a[0][j] = (s02 + s13, None)
        a[4][j] = (s02 - s13, None)
        a[2][j] = (x0 - x2, x3 - x1)
        a[1][j] = (x0 + d, -(x2 + e))
        a[3][j] = (x0 - d, x2 - e)
    out = [None] * 33
    for p in range(5):
        b = [a[p][j] if p * j == 0 else times(a[p][j], -2.0 * math.pi * p * j / 64) for j in range(8)]
        f = fft8(b, -1)
        for q in range(8):
            k = p + 8 * q
            if k <= 32:
                out[k] = f[q]
            elif 1 <= p <= 3:
                out[64 - k] = conj(f[q])
    return out


def join_rows(q):
    y = [None] * 32
    b = []
    for p in range(5):
        v = [q[p + 8 * i] if p + 8 * i <= 32 else conj(q[64 - p - 8 * i]) for i in range(8)]
        f = fft8(v, 1)
        b.append([f[j] if p * j == 0 else times(f[j], 2.0 * math.pi * p * j / 64) for j in range(8)])
    for j in range(8):
        b0, b4 = b[0][j][0], b[4][j][0]
        even, odd = 0.5 * (b0 + b4), 0.5 * (b0 - b4)
        (r1, i1), (r2, i2), (r3, i3) = b[1][j], b[2][j], b[3][j]
        y[j] = even + r2 + (r1 + r3)
        y[16 + j] = even - r2 + (i3 - i1)
        u, w = R2 * (r1 - r3), R2 * (i1 + i3)
        y[8 + j] = odd - i2 + (u - w)
        y[24 + j] = odd + i2 - (u + w)
    return y


def spectrum_kernel(
    filt_ref, mix_ref, scl_ref, cos_ref, sin_ref, wc_ref, ws_ref, wct_ref, wst_ref,
    conv_out, back_out, fg_out,
    spec, back_spec, tr, ti, er, ei, fwd, inv, wide,
):
    def first(block, carry):
        rows = pl.ds(pl.multiple_of(block * 16, 16), 16)
        for half in range(2):
            lo = 8 * half
            at = pl.multiple_of(block * 16 + lo, 8)
            for index, source in ((0, mix_ref), (1, scl_ref), (2, None)):
                if source is None:
                    x = [filt_ref[pl.ds(at, 8), n * 128 : (n + 1) * 128] for n in range(32)]
                else:
                    x = [source[n, rows].astype(F32)[lo : lo + 8] for n in range(32)]
                to = pl.ds(pl.multiple_of(index * CH + at, 8), 8)
                for k, (re, im) in enumerate(split_rows(x)):
                    spec[k, to, 0:128] = re
                    spec[k, to, 128:256] = jnp.zeros_like(re) if im is None else im
        return carry

    lax.fori_loop(0, CH // 16, first, 0)

    scale = 2.0 / 8192
    tr[...] = cos_ref[...]
    ti[...] = -sin_ref[...]
    er[...] = cos_ref[...] * scale
    ei[...] = sin_ref[...] * scale

    def second(k, carry):
        a, b = tr[...], ti[...]
        fwd[0:128, 0:128] = a.astype(BF)
        fwd[128:256, 128:256] = a.astype(BF)
        fwd[0:128, 128:256] = b.astype(BF)
        fwd[128:256, 0:128] = (-b).astype(BF)
        c, s = wc_ref[...], ws_ref[...]
        tr[...] = a * c + b * s
        ti[...] = b * c - a * s
        a, b = er[...], ei[...]
        inv[0:128, 0:128] = a.astype(BF)
        inv[128:256, 128:256] = a.astype(BF)
        inv[0:128, 128:256] = b.astype(BF)
        inv[128:256, 0:128] = (-b).astype(BF)
        c, s = wct_ref[...], wst_ref[...]
        er[...] = a * c - b * s
        ei[...] = b * c + a * s
        full = jnp.dot(spec[k].astype(BF), fwd[...], preferred_element_type=F32)
        mr, mi = full[0:CH, 0:128], full[0:CH, 128:256]
        gr, gi = full[CH : 2 * CH, 0:128], full[CH : 2 * CH, 128:256]
        fr, fi = full[2 * CH : 3 * CH, 0:128], full[2 * CH : 3 * CH, 128:256]
        wide[0:CH, 0:128] = (fr * mr - fi * mi).astype(BF)
        wide[0:CH, 128:256] = (fr * mi + fi * mr).astype(BF)
        wide[CH : 2 * CH, 0:128] = (fr * gr + fi * gi).astype(BF)
        wide[CH : 2 * CH, 128:256] = (fr * gi - fi * gr).astype(BF)
        wide[2 * CH : 3 * CH, 0:128] = (mr * gr + mi * gi).astype(BF)
        wide[2 * CH : 3 * CH, 128:256] = (mr * gi - mi * gr).astype(BF)
        back_spec[k] = jnp.dot(wide[...], inv[...], preferred_element_type=F32)
        return carry

    lax.fori_loop(0, 33, second, 0)

    def third(block, carry):
        rows = pl.ds(pl.multiple_of(block * 16, 16), 16)
        for index, target in ((0, conv_out), (1, back_out), (2, None)):
            halves = []
            for half in range(2):
                to = pl.ds(pl.multiple_of(index * CH + block * 16 + 8 * half, 8), 8)
                q = [(back_spec[k, to, 0:128], back_spec[k, to, 128:256]) for k in range(33)]
                halves.append(join_rows(q))
            for n in range(32):
                value = jnp.concatenate([halves[0][n], halves[1][n]], axis=0).astype(BF)
                if target is None:
                    fg_out[rows, n * 128 : (n + 1) * 128] = value
                else:
                    target[n, rows] = value
        return carry

    lax.fori_loop(0, CH // 16, third, 0)


def spectrum_call(filters, mixed, scaled):
    i = np.arange(128)
    angle = 2.0 * np.pi * ((i[:, None] * i[None, :]) % 128) / 128
    step = np.broadcast_to((2.0 * np.pi * i / 8192)[:, None], (128, 128))
    tables = [np.cos(angle), np.sin(angle), np.cos(step), np.sin(step), np.cos(step.T), np.sin(step.T)]
    tables = [jnp.asarray(np.ascontiguousarray(t), F32) for t in tables]
    vmem = pl.BlockSpec(memory_space=pltpu.VMEM)
    return pl.pallas_call(
        spectrum_kernel,
        name="spectrum",
        out_shape=[
            jax.ShapeDtypeStruct((32, CH, 128), BF),
            jax.ShapeDtypeStruct((32, CH, 128), BF),
            jax.ShapeDtypeStruct((CH, 4096), BF),
        ],
        in_specs=[vmem] * 9,
        out_specs=[vmem] * 3,
        scratch_shapes=[
            pltpu.VMEM((33, 3 * CH, 256), F32),
            pltpu.VMEM((33, 3 * CH, 256), F32),
        ]
        + [pltpu.VMEM((128, 128), F32)] * 4
        + [pltpu.VMEM((256, 256), BF)] * 2
        + [pltpu.VMEM((3 * CH, 256), BF)],
        compiler_params=pltpu.CompilerParams(vmem_limit_bytes=48 << 20),
    )(filters, mixed, scaled, *tables)


def per_device(queries, keys, values, upstream, filters, out_weight, middle=spectrum_call):
    nctx, nnear = NZH * NY * NC, NY * NC
    key_rows, value_rows = keys[0], values[0]
    mixed = (key_rows.astype(F32) * value_rows.astype(F32)).astype(BF)
    mixed_t = mixed.T.reshape(nctx, CH, TOK)
    query_t = queries[0].T.reshape(NZH, nnear, CH, TOK)
    mix_chan, scl_chan, gg, query, up = gather_call(mixed_t, query_t, upstream[0], out_weight)
    conv, back, fg = middle(filters, mix_chan, scl_chan)
    gq, back, fg, gw = scatter_call(conv, back, fg, gg, query, up)
    grad_queries = gq.reshape(nctx * CH, TOK).T
    back_wide = back.reshape(nctx * CH, TOK).T.astype(F32)
    grad_keys = (back_wide * value_rows.astype(F32)).astype(BF)
    grad_values = (back_wide * key_rows.astype(F32)).astype(BF)
    return (grad_queries[None], grad_keys[None], grad_values[None], fg.astype(F32), gw.astype(F32))


def solution(mesh):
    rows = P("dp", "ctx", None)
    chans = P("ctx", None)
    return jax.shard_map(
        per_device,
        mesh=mesh,
        in_specs=(rows, rows, rows, rows, chans, chans),
        out_specs=(rows, rows, rows, chans, chans),
        check_vma=False,
    )
```

```python
import functools
import math

import jax
import jax.numpy as jnp
import numpy as np
from jax import lax
from jax.experimental import pallas as pl
from jax.experimental.pallas import tpu as pltpu
from jax.sharding import PartitionSpec as P

NX, NZL, NZH, NY, NC = 4, 2, 4, 4, 2
TOK, CH = 128, 64
BF, F32 = jnp.bfloat16, jnp.float32
MESH = pl.DeviceIdType.MESH


def place():
    dp = lax.axis_index("dp")
    ctx = lax.axis_index("ctx")
    near = NY * NC
    return dict(
        dp=dp,
        ctx=ctx,
        x=lax.rem(dp, NX),
        zl=dp // NX,
        zh=ctx // near,
        near=lax.rem(ctx, near),
        y=lax.rem(ctx, near) // NC,
        core=lax.rem(ctx, NC),
    )


def send(src, dst, ssem, rsem, dp, ctx):
    return pltpu.make_async_remote_copy(
        src_ref=src,
        dst_ref=dst,
        send_sem=ssem,
        recv_sem=rsem,
        device_id=(dp, ctx),
        device_id_type=MESH,
    )


R2 = math.sqrt(0.5)


def add(a, b):
    return tuple(p if q is None else q if p is None else p + q for p, q in zip(a, b))


def neg(a):
    return tuple(None if p is None else -p for p in a)


def sub(a, b):
    return tuple(
        p if q is None else -q if p is None else p - q for p, q in zip(a, b)
    )


def conj(a):
    return (a[0], None if a[1] is None else -a[1])


def turn(a):
    return (None if a[1] is None else -a[1], a[0])


def unturn(a):
    return (a[1], None if a[0] is None else -a[0])


def times(a, angle):
    c, s = math.cos(angle), math.sin(angle)
    if a[1] is None:
        return (a[0] * c, a[0] * s)
    return (a[0] * c - a[1] * s, a[0] * s + a[1] * c)


def fft4(a, b, c, d, sign):
    s0, s1, s2, s3 = add(a, c), sub(a, c), add(b, d), sub(b, d)
    t3 = turn(s3) if sign > 0 else unturn(s3)
    return [add(s0, s2), add(s1, t3), sub(s0, s2), sub(s1, t3)]


def eighth(a, sign):
    if a[1] is None:
        return (a[0] * R2, a[0] * (R2 * sign))
    if sign > 0:
        return ((a[0] - a[1]) * R2, (a[0] + a[1]) * R2)
    return ((a[0] + a[1]) * R2, (a[1] - a[0]) * R2)


def fft8(v, sign):
    even = fft4(v[0], v[2], v[4], v[6], sign)
    odd = fft4(v[1], v[3], v[5], v[7], sign)
    quarter = turn if sign > 0 else unturn
    odd = [odd[0], eighth(odd[1], sign), quarter(odd[2]), quarter(eighth(odd[3], sign))]
    return [add(e, o) for e, o in zip(even, odd)] + [sub(e, o) for e, o in zip(even, odd)]


def split_rows(x):
    a = [[None] * 8 for _ in range(5)]
    for j in range(8):
        x0, x1, x2, x3 = x[j], x[8 + j], x[16 + j], x[24 + j]
        d, e = (x1 - x3) * R2, (x1 + x3) * R2
        s02, s13 = x0 + x2, x1 + x3
        a[0][j] = (s02 + s13, None)
        a[4][j] = (s02 - s13, None)
        a[2][j] = (x0 - x2, x3 - x1)
        a[1][j] = (x0 + d, -(x2 + e))
        a[3][j] = (x0 - d, x2 - e)
    out = [None] * 33
    for p in range(5):
        b = [a[p][j] if p * j == 0 else times(a[p][j], -2.0 * math.pi * p * j / 64) for j in range(8)]
        f = fft8(b, -1)
        for q in range(8):
            k = p + 8 * q
            if k <= 32:
                out[k] = f[q]
            elif 1 <= p <= 3:
                out[64 - k] = conj(f[q])
    return out


def join_rows(q):
    y = [None] * 32
    b = []
    for p in range(5):
        v = [q[p + 8 * i] if p + 8 * i <= 32 else conj(q[64 - p - 8 * i]) for i in range(8)]
        f = fft8(v, 1)
        b.append([f[j] if p * j == 0 else times(f[j], 2.0 * math.pi * p * j / 64) for j in range(8)])
    for j in range(8):
        b0, b4 = b[0][j][0], b[4][j][0]
        even, odd = 0.5 * (b0 + b4), 0.5 * (b0 - b4)
        (r1, i1), (r2, i2), (r3, i3) = b[1][j], b[2][j], b[3][j]
        y[j] = even + r2 + (r1 + r3)
        y[16 + j] = even - r2 + (i3 - i1)
        u, w = R2 * (r1 - r3), R2 * (i1 + i3)
        y[8 + j] = odd - i2 + (u - w)
        y[24 + j] = odd + i2 - (u + w)
    return y


def mixer_kernel(
    key_ref, value_ref, query_ref, up_ref, filt_ref, w_ref,
    cos_ref, sin_ref, wc_ref, ws_ref, wct_ref, wst_ref,
    gq_out, back_out, fg_out, gw_out,
    k_own, v_own, q_own, f_own, mix_t, q_t, mix_all, q_all, up_all, w_all, gg_all, sc_all, scl_all,
    ft, it, tab, part, filt_s, mix_s, iq, conv_own, conv_all, back_own, fg_own, gate, gq_all,
    fg_x, fg_half, fg_z, fg_fin, gw_part, gw_x, gw_mid, gw_z, gw_fin,
    m_send, m_recv, u_send, u_recv, r_send, r_recv, p_send, p_recv, q_send, q_recv,
    w_send, w_recv, v_send, v_recv, s_send, s_recv, c_send, c_recv, b_send, b_recv,
    fx_send, fx_recv, fz_send, fz_recv, fa_send, fa_recv,
    g_send, g_recv, wx_send, wx_recv, wz_send, wz_recv, wa_send, wa_recv, local,
):
    at = place()
    dp, ctx, near, zh, zl, x = (at[k] for k in ("dp", "ctx", "near", "zh", "zl", "x"))
    y, core = at["y"], at["core"]
    nctx, nnear, ndp, nz = NZH * NY * NC, NY * NC, NX * NZL, NZH * NZL
    rows = CH // NX
    depth = up_ref.shape[-1]
    seq = nctx * TOK
    span = seq // NZL
    wide, narrow = depth // NX, depth // NX // NZL
    half = TOK // 2

    peers = [(dp, lax.rem(ctx + s, nctx)) for s in range(1, nctx)]
    peers += [(lax.rem(dp + s, ndp), ctx) for s in range(1, ndp)]
    other = lax.rem(zl + 1, NZL) * NX + x
    if NZL > 1:
        peers += [(other, lax.rem(zh + s, NZH) * nnear + near) for s in range(1, NZH)]
    barrier = pltpu.get_barrier_semaphore()
    for d, c in peers:
        pl.semaphore_signal(barrier, inc=1, device_id=(d, c), device_id_type=MESH)
    loads = [
        pltpu.make_async_copy(key_ref, k_own, local.at[0]),
        pltpu.make_async_copy(value_ref, v_own, local.at[1]),
        pltpu.make_async_copy(query_ref, q_own, local.at[2]),
        pltpu.make_async_copy(filt_ref, f_own, local.at[3]),
        pltpu.make_async_copy(up_ref, up_all.at[near], local.at[4]),
        pltpu.make_async_copy(w_ref, w_all.at[zh], local.at[5]),
    ]
    for copy in loads:
        copy.start()
    loads[0].wait()
    loads[1].wait()

    def mix_block(j, carry):
        cols = pl.ds(pl.multiple_of(j * 2 * CH, 2 * CH), 2 * CH)
        mixed = (k_own[:, cols].astype(F32) * v_own[:, cols].astype(F32)).astype(BF)
        turned = mixed.astype(F32).T.astype(BF)
        mix_t[2 * j] = turned[0:CH]
        mix_t[2 * j + 1] = turned[CH : 2 * CH]
        return carry

    lax.fori_loop(0, nctx // 2, mix_block, 0)
    mix_all[ctx] = mix_t[ctx]
    pl.semaphore_wait(barrier, len(peers))

    ms = []
    for s in range(1, nctx):
        to = lax.rem(ctx + s, nctx)
        ms.append(send(mix_t.at[to], mix_all.at[ctx], m_send.at[s], m_recv.at[s], dp, to))
        ms[-1].start()
    mine = pl.ds(pl.multiple_of(x * rows, rows), rows)
    ws = []
    for s in range(1, NZH):
        there = lax.rem(zh + s, NZH) * nnear + near
        ws.append(send(w_ref.at[mine], w_all.at[zh, mine], w_send.at[s], w_recv.at[s], dp, there))
        ws[-1].start()

    def along_y(step):
        return zh * nnear + lax.rem(y + step + NY, NY) * NC + core

    def slot_of(step, dc):
        return lax.rem(y + step + NY, NY) * NC + lax.rem(core + dc, NC)

    partner = zh * nnear + y * NC + lax.rem(core + 1, NC)
    steps = {4: (1, -1), 2: (1,), 1: ()}[NY]
    us = {}
    for order in range(2):
        for step in steps:
            h = order if step > 0 else 1 - order
            piece = pl.ds(h * half, half)
            i = (0 if step > 0 else 1) * 2 + h
            us[step, h] = send(
                up_ref.at[piece], up_all.at[near, piece], u_send.at[i], u_recv.at[i], dp, along_y(step)
            )
            us[step, h].start()
    pair = send(up_ref, up_all.at[near], p_send.at[0], p_recv.at[0], dp, partner)
    pair.start()

    loads[2].wait()

    def query_block(j, carry):
        cols = pl.ds(pl.multiple_of(j * 2 * CH, 2 * CH), 2 * CH)
        turned = q_own[:, cols].astype(F32).T.astype(BF)
        first = 2 * j
        q_t[lax.rem(first, nnear), first // nnear] = turned[0:CH]
        q_t[lax.rem(first + 1, nnear), (first + 1) // nnear] = turned[CH : 2 * CH]
        return carry

    lax.fori_loop(0, nctx // 2, query_block, 0)
    qs = []
    for s in range(1, nnear):
        to = lax.rem(near + s, nnear)
        qs.append(send(q_t.at[to], q_all.at[near], q_send.at[s], q_recv.at[s], dp, zh * nnear + to))
        qs[-1].start()
    q_all[near] = q_t[near]

    scale = 2.0 / 8192
    tab[0] = cos_ref[...]
    tab[1] = -sin_ref[...]
    tab[2] = cos_ref[...] * scale
    tab[3] = sin_ref[...] * scale

    def build(k, carry):
        a, b = tab[0], tab[1]
        ft[k, 0:128, 0:128] = a.astype(BF)
        ft[k, 128:256, 128:256] = a.astype(BF)
        ft[k, 0:128, 128:256] = b.astype(BF)
        ft[k, 128:256, 0:128] = (-b).astype(BF)
        c, s = wc_ref[...], ws_ref[...]
        tab[0] = a * c + b * s
        tab[1] = b * c - a * s
        a, b = tab[2], tab[3]
        it[k, 0:128, 0:128] = a.astype(BF)
        it[k, 128:256, 128:256] = a.astype(BF)
        it[k, 0:128, 128:256] = b.astype(BF)
        it[k, 128:256, 0:128] = (-b).astype(BF)
        c, s = wct_ref[...], wst_ref[...]
        tab[2] = a * c - b * s
        tab[3] = b * c + a * s
        return carry

    lax.fori_loop(0, 33, build, 0)

    def sections(source):
        def body(block, carry):
            at16 = pl.ds(pl.multiple_of(block * 16, 16), 16)
            for lo in (0, 8):
                to = pl.ds(pl.multiple_of(block * 16 + lo, 8), 8)
                if source is None:
                    v = [f_own[to, n * TOK : (n + 1) * TOK] for n in range(nctx)]
                else:
                    v = [source[n, at16].astype(F32)[lo : lo + 8] for n in range(nctx)]
                v += [jnp.zeros_like(v[0])] * (32 - nctx)
                for k, (re, im) in enumerate(split_rows(v)):
                    part[k, to, 0:128] = re
                    part[k, to, 128:256] = jnp.zeros_like(re) if im is None else im
            return carry

        lax.fori_loop(0, CH // 16, body, 0)

    def rejoin(lo_row, target):
        def body(block, carry):
            at16 = pl.ds(pl.multiple_of(block * 16, 16), 16)
            halves = []
            for lo in (0, 8):
                to = pl.ds(pl.multiple_of(lo_row + block * 16 + lo, 8), 8)
                halves.append(
                    join_rows([(iq[k, to, 0:128], iq[k, to, 128:256]) for k in range(33)])
                )
            for n in range(nctx):
                value = jnp.concatenate([halves[0][n], halves[1][n]], axis=0).astype(BF)
                if target is fg_own:
                    target[at16, n * TOK : (n + 1) * TOK] = value
                else:
                    target[n, at16] = value
            return carry

        lax.fori_loop(0, CH // 16, body, 0)

    def forward(k):
        full = jnp.dot(part[k].astype(BF), ft[k], preferred_element_type=F32)
        return full[:, 0:128], full[:, 128:256]

    loads[3].wait()
    sections(None)

    vs = []
    for s, copy in enumerate(ws, 1):
        copy.wait_recv()
        shard = lax.rem(zh + NZH - s, NZH)
        for t in range(1, NX):
            there = zl * NX + lax.rem(x + t, NX)
            piece = w_all.at[shard, mine]
            vs.append(send(piece, piece, v_send.at[s, t], v_recv.at[s, t], there, ctx))
            vs[-1].start()
    rs = []
    if NY == 4:
        for step, h in ((1, 0), (-1, 1)):
            us[step, h].wait_recv()
            piece = up_all.at[slot_of(-step, 0), pl.ds(h * half, half)]
            rs.append(send(piece, piece, r_send.at[h], r_recv.at[h], dp, along_y(step)))
            rs[-1].start()

    def filter_step(k, carry):
        re, im = forward(k)
        filt_s[k, :, 0:128] = re
        filt_s[k, :, 128:256] = im
        return carry

    lax.fori_loop(0, 33, filter_step, 0)

    relays = []

    def relay(slot, index):
        piece = up_all.at[slot]
        relays.append(send(piece, piece, p_send.at[index], p_recv.at[index], dp, partner))
        relays[-1].start()

    for i, step in enumerate(steps):
        for h in range(2):
            if not (NY == 4 and (step, h) in ((1, 0), (-1, 1))):
                us[step, h].wait_recv()
        relay(slot_of(-step, 0), 1 + i)

    for copy in ms:
        copy.wait_recv()
    sections(mix_all)

    def conv_step(k, carry):
        mr, mi = forward(k)
        mix_s[k, :, 0:128] = mr
        mix_s[k, :, 128:256] = mi
        fr, fi = filt_s[k, :, 0:128], filt_s[k, :, 128:256]
        both = jnp.concatenate([fr * mr - fi * mi, fr * mi + fi * mr], axis=1).astype(BF)
        iq[k, 0:CH] = jnp.dot(both, it[k], preferred_element_type=F32)
        return carry

    lax.fori_loop(0, 33, conv_step, 0)
    rejoin(0, conv_own)
    cs = []
    for s in range(1, NZH):
        to = lax.rem(zh + s, NZH)
        cs.append(
            send(
                conv_own.at[pl.ds(to * nnear, nnear)], conv_all.at[zh],
                c_send.at[s], c_recv.at[s], dp, to * nnear + near,
            )
        )
        cs[-1].start()
    for i in range(nnear):
        conv_all[zh, i] = conv_own[zh * nnear + i]

    far = slot_of(2, 0)
    if NY == 4:
        for copy in rs:
            copy.wait_recv()
        relay(far, 3)
    loads[4].wait()
    loads[5].wait()
    for copy in vs + qs:
        copy.wait_recv()
    ss = []

    def work(slot, k):
        w = w_all[...].reshape(NZH * CH, depth)
        gg = lax.dot_general(
            w, up_all[slot], (((1,), (1,)), ((), ())), preferred_element_type=F32
        ).astype(BF)
        gg = gg.reshape(NZH, CH, TOK)
        gg_all[slot] = gg
        sc_all[slot] = (gg.astype(F32) * q_all[slot].astype(F32)).astype(BF)
        n = zh * nnear + slot
        for s in range(1, NZH):
            to = lax.rem(zh + s, NZH)
            ss.append(
                send(
                    sc_all.at[slot, to], scl_all.at[n],
                    s_send.at[k, s], s_recv.at[k, s], dp, to * nnear + near,
                )
            )
            ss[-1].start()
        scl_all[n] = sc_all[slot, zh]

    work(near, 0)
    for i, step in enumerate(steps):
        work(slot_of(-step, 0), 1 + i)
    pair.wait_recv()
    work(slot_of(0, 1), NY)
    for i, step in enumerate(steps):
        relays[i].wait_recv()
        work(slot_of(-step, 1), NY + 1 + i)
    if NY == 4:
        work(far, 3)
        relays[2].wait_recv()
        work(slot_of(2, 1), 7)

    for copy in cs:
        copy.wait_recv()
    for i in range(nnear):
        for h in range(NZH):
            conv = conv_all[h, i].astype(F32)
            gq_all[i, h] = (gg_all[i, h].astype(F32) * conv).astype(BF)
            gate[h * CH : (h + 1) * CH, i * TOK : (i + 1) * TOK] = (
                q_all[i, h].astype(F32) * conv
            ).astype(BF)
    wxs = []
    for s in list(range(1, NX)) + [0]:
        to = lax.rem(x + s, NX)
        cols = pl.ds(pl.multiple_of(to * wide, wide), wide)
        up = up_all[:, :, cols].reshape(nnear * TOK, wide)
        gw_part[to] = jnp.dot(gate[...], up, preferred_element_type=F32).astype(BF)
        if s:
            wxs.append(
                send(gw_part.at[to], gw_x.at[x], wx_send.at[s], wx_recv.at[s], zl * NX + to, ctx)
            )
            wxs[-1].start()
    gw_x[x] = gw_part[x]
    gs = []
    for s in range(1, nnear):
        to = lax.rem(near + s, nnear)
        gs.append(
            send(gq_all.at[to], gq_out.at[:, near], g_send.at[s], g_recv.at[s], dp, zh * nnear + to)
        )
        gs[-1].start()
    own_g = pltpu.make_async_copy(gq_all.at[near], gq_out.at[:, near], local.at[7])
    own_g.start()

    for copy in ss:
        copy.wait_recv()
    sections(scl_all)

    def back_step(k, carry):
        gr, gi = forward(k)
        fr, fi = filt_s[k, :, 0:128], filt_s[k, :, 128:256]
        mr, mi = mix_s[k, :, 0:128], mix_s[k, :, 128:256]
        upper = jnp.concatenate([fr * gr + fi * gi, fr * gi - fi * gr], axis=1).astype(BF)
        lower = jnp.concatenate([mr * gr + mi * gi, mr * gi - mi * gr], axis=1).astype(BF)
        both = jnp.concatenate([upper, lower], axis=0)
        iq[k] = jnp.dot(both, it[k], preferred_element_type=F32)
        return carry

    lax.fori_loop(0, 33, back_step, 0)
    rejoin(0, back_own)
    bs = []
    for s in range(1, nctx):
        to = lax.rem(ctx + s, nctx)
        bs.append(send(back_own.at[to], back_out.at[ctx], b_send.at[s], b_recv.at[s], dp, to))
        bs[-1].start()
    own_b = pltpu.make_async_copy(back_own.at[ctx], back_out.at[ctx], local.at[8])
    own_b.start()
    rejoin(CH, fg_own)
    fxs = []
    for s in range(1, NX):
        to = lax.rem(x + s, NX)
        fxs.append(
            send(
                fg_own.at[pl.ds(pl.multiple_of(to * rows, rows), rows)], fg_x.at[x],
                fx_send.at[s], fx_recv.at[s], zl * NX + to, ctx,
            )
        )
        fxs[-1].start()
    fg_x[x] = fg_own[mine]

    for copy in wxs:
        copy.wait_recv()
    for h in range(NZH):
        total = gw_x[0, h * CH : (h + 1) * CH].astype(F32)
        for i in range(1, NX):
            total = total + gw_x[i, h * CH : (h + 1) * CH].astype(F32)
        for i in range(NZL):
            gw_mid[h, i] = total[:, i * narrow : (i + 1) * narrow].astype(BF)
    zs = []
    for s in range(NZH):
        for l in range(NZL):
            if s or l:
                to, tl = lax.rem(zh + s, NZH), lax.rem(zl + l, NZL)
                k = s * NZL + l
                zs.append(
                    send(
                        gw_mid.at[to, tl], gw_z.at[zh * NZL + zl],
                        wz_send.at[k], wz_recv.at[k], tl * NX + x, to * nnear + near,
                    )
                )
                zs[-1].start()
    gw_z[zh * NZL + zl] = gw_mid[zh, zl]

    for copy in fxs:
        copy.wait_recv()
    total = fg_x[0].astype(F32)
    for i in range(1, NX):
        total = total + fg_x[i].astype(F32)
    for i in range(NZL):
        fg_half[i] = total[:, i * span : (i + 1) * span].astype(BF)
    fzs = []
    for s in range(1, NZL):
        to = lax.rem(zl + s, NZL)
        fzs.append(
            send(fg_half.at[to], fg_z.at[zl], fz_send.at[s], fz_recv.at[s], to * NX + x, ctx)
        )
        fzs[-1].start()
    fg_z[zl] = fg_half[zl]

    for copy in zs:
        copy.wait_recv()
    total = gw_z[0].astype(F32)
    for i in range(1, nz):
        total = total + gw_z[i].astype(F32)
    gw_fin[...] = total.astype(BF)
    was = []
    wslot = gw_out.at[:, pl.ds(pl.multiple_of((x * NZL + zl) * narrow, narrow), narrow)]
    for s in range(1, ndp):
        to = lax.rem(dp + s, ndp)
        was.append(send(gw_fin, wslot, wa_send.at[s], wa_recv.at[s], to, ctx))
        was[-1].start()
    own_wa = pltpu.make_async_copy(gw_fin, wslot, local.at[9])
    own_wa.start()

    for copy in fzs:
        copy.wait_recv()
    total = fg_z[0].astype(F32)
    for i in range(1, NZL):
        total = total + fg_z[i].astype(F32)
    fg_fin[...] = total.astype(BF)
    fas = []
    fslot = fg_out.at[mine, pl.ds(pl.multiple_of(zl * span, span), span)]
    for s in range(1, ndp):
        to = lax.rem(dp + s, ndp)
        fas.append(send(fg_fin, fslot, fa_send.at[s], fa_recv.at[s], to, ctx))
        fas[-1].start()
    own_fa = pltpu.make_async_copy(fg_fin, fslot, local.at[10])
    own_fa.start()

    for copy in (own_g, own_b, own_wa, own_fa):
        copy.wait()
    sent = ms + ws + list(us.values()) + [pair] + qs + vs + rs + relays + cs + ss
    for copy in sent + wxs + fxs + fzs + zs:
        copy.wait_send()
    for copy in gs + bs + was + fas:
        copy.wait()


def mixer_call(keys, values, queries, up, filters, w):
    nctx, nnear, ndp, nz = NZH * NY * NC, NY * NC, NX * NZL, NZH * NZL
    depth = up.shape[-1]
    seq = nctx * TOK
    wide, narrow = depth // NX, depth // NX // NZL
    rows, span = CH // NX, seq // NZL
    i = np.arange(128)
    angle = 2.0 * np.pi * ((i[:, None] * i[None, :]) % 128) / 128
    step = np.broadcast_to((2.0 * np.pi * i / 8192)[:, None], (128, 128))
    tables = [np.cos(angle), np.sin(angle), np.cos(step), np.sin(step), np.cos(step.T), np.sin(step.T)]
    tables = [jnp.asarray(np.ascontiguousarray(t), F32) for t in tables]
    dma = pltpu.SemaphoreType.DMA
    hbm = pl.BlockSpec(memory_space=pl.ANY)
    vmem = pl.BlockSpec(memory_space=pltpu.VMEM)
    near4 = (nnear, NZH, CH, TOK)
    chans = (nctx, CH, TOK)
    spec = (33, CH, 256)
    pairs = [
        (nctx,), (4,), (2,), (4,), (nnear,), (NZH,), (NZH, NX), (nnear, NZH), (NZH,), (nctx,),
        (NX,), (NZL,), (ndp,), (nnear,), (NX,), (nz,), (ndp,),
    ]
    return pl.pallas_call(
        mixer_kernel,
        name="mixer",
        out_shape=[
            jax.ShapeDtypeStruct((NZH, nnear, CH, TOK), BF),
            jax.ShapeDtypeStruct(chans, BF),
            jax.ShapeDtypeStruct((CH, seq), BF),
            jax.ShapeDtypeStruct((CH, depth), BF),
        ],
        in_specs=[hbm] * 6 + [vmem] * 6,
        out_specs=[hbm] * 4,
        scratch_shapes=[
            pltpu.VMEM((TOK, nctx * CH), BF),
            pltpu.VMEM((TOK, nctx * CH), BF),
            pltpu.VMEM((TOK, nctx * CH), BF),
            pltpu.VMEM((CH, seq), F32),
            pltpu.VMEM(chans, BF),
            pltpu.VMEM(near4, BF),
            pltpu.VMEM(chans, BF),
            pltpu.VMEM(near4, BF),
            pltpu.VMEM((nnear, TOK, depth), BF),
            pltpu.VMEM((NZH, CH, depth), BF),
            pltpu.VMEM(near4, BF),
            pltpu.VMEM(near4, BF),
            pltpu.VMEM(chans, BF),
            pltpu.VMEM((33, 256, 256), BF),
            pltpu.VMEM((33, 256, 256), BF),
            pltpu.VMEM((4, 128, 128), F32),
            pltpu.VMEM(spec, F32),
            pltpu.VMEM(spec, F32),
            pltpu.VMEM(spec, F32),
            pltpu.VMEM((33, 2 * CH, 256), F32),
            pltpu.VMEM(chans, BF),
            pltpu.VMEM((NZH, nnear, CH, TOK), BF),
            pltpu.VMEM(chans, BF),
            pltpu.VMEM((CH, seq), BF),
            pltpu.VMEM((NZH * CH, nnear * TOK), BF),
            pltpu.VMEM(near4, BF),
            pltpu.VMEM((NX, rows, seq), BF),
            pltpu.VMEM((NZL, rows, span), BF),
            pltpu.VMEM((NZL, rows, span), BF),
            pltpu.VMEM((rows, span), BF),
            pltpu.VMEM((NX, NZH * CH, wide), BF),
            pltpu.VMEM((NX, NZH * CH, wide), BF),
            pltpu.VMEM((NZH, NZL, CH, narrow), BF),
            pltpu.VMEM((nz, CH, narrow), BF),
            pltpu.VMEM((CH, narrow), BF),
        ]
        + [dma(n) for n in pairs for _ in range(2)]
        + [dma((12,))],
        compiler_params=pltpu.CompilerParams(
            collective_id=0, has_side_effects=True, vmem_limit_bytes=60 << 20
        ),
    )(keys, values, queries, up, filters, w, *tables)


def per_device(queries, keys, values, upstream, filters, out_weight):
    nctx = NZH * NY * NC
    key_rows, value_rows = keys[0], values[0]
    gq, back, fg, gw = mixer_call(
        key_rows, value_rows, queries[0], upstream[0], filters, out_weight
    )
    grad_queries = gq.reshape(nctx * CH, TOK).T
    back_wide = back.reshape(nctx * CH, TOK).T.astype(F32)
    grad_keys = (back_wide * value_rows.astype(F32)).astype(BF)
    grad_values = (back_wide * key_rows.astype(F32)).astype(BF)
    return (grad_queries[None], grad_keys[None], grad_values[None], fg.astype(F32), gw.astype(F32))


def solution(mesh):
    rows = P("dp", "ctx", None)
    chans = P("ctx", None)
    return jax.shard_map(
        per_device,
        mesh=mesh,
        in_specs=(rows, rows, rows, rows, chans, chans),
        out_specs=(rows, rows, rows, chans, chans),
        check_vma=False,
    )
```

```python
import functools
import math

import jax
import jax.numpy as jnp
import numpy as np
from jax import lax
from jax.experimental import pallas as pl
from jax.experimental.pallas import tpu as pltpu
from jax.sharding import PartitionSpec as P

NX, NZL, NZH, NY, NC = 4, 2, 4, 4, 2
TOK, CH = 128, 64
HALF = CH // 2
UNROLL = 11
BF, F32 = jnp.bfloat16, jnp.float32
MESH = pl.DeviceIdType.MESH


def drain(view, sem):
    pltpu.make_async_copy(view, view, sem).wait()


def place():
    dp = lax.axis_index("dp")
    ctx = lax.axis_index("ctx")
    near = NY * NC
    return dict(
        dp=dp,
        ctx=ctx,
        x=lax.rem(dp, NX),
        zl=dp // NX,
        zh=ctx // near,
        near=lax.rem(ctx, near),
        y=lax.rem(ctx, near) // NC,
        core=lax.rem(ctx, NC),
    )


def send(src, dst, ssem, rsem, dp, ctx):
    return pltpu.make_async_remote_copy(
        src_ref=src,
        dst_ref=dst,
        send_sem=ssem,
        recv_sem=rsem,
        device_id=(dp, ctx),
        device_id_type=MESH,
    )


R2 = math.sqrt(0.5)


def add(a, b):
    return tuple(p if q is None else q if p is None else p + q for p, q in zip(a, b))


def neg(a):
    return tuple(None if p is None else -p for p in a)


def sub(a, b):
    return tuple(
        p if q is None else -q if p is None else p - q for p, q in zip(a, b)
    )


def conj(a):
    return (a[0], None if a[1] is None else -a[1])


def turn(a):
    return (None if a[1] is None else -a[1], a[0])


def unturn(a):
    return (a[1], None if a[0] is None else -a[0])


def times(a, angle):
    c, s = math.cos(angle), math.sin(angle)
    if a[1] is None:
        return (a[0] * c, a[0] * s)
    return (a[0] * c - a[1] * s, a[0] * s + a[1] * c)


def fft4(a, b, c, d, sign):
    s0, s1, s2, s3 = add(a, c), sub(a, c), add(b, d), sub(b, d)
    t3 = turn(s3) if sign > 0 else unturn(s3)
    return [add(s0, s2), add(s1, t3), sub(s0, s2), sub(s1, t3)]


def eighth(a, sign):
    if a[1] is None:
        return (a[0] * R2, a[0] * (R2 * sign))
    if sign > 0:
        return ((a[0] - a[1]) * R2, (a[0] + a[1]) * R2)
    return ((a[0] + a[1]) * R2, (a[1] - a[0]) * R2)


def fft8(v, sign):
    even = fft4(v[0], v[2], v[4], v[6], sign)
    odd = fft4(v[1], v[3], v[5], v[7], sign)
    quarter = turn if sign > 0 else unturn
    odd = [odd[0], eighth(odd[1], sign), quarter(odd[2]), quarter(eighth(odd[3], sign))]
    return [add(e, o) for e, o in zip(even, odd)] + [sub(e, o) for e, o in zip(even, odd)]


def split_rows(x):
    a = [[None] * 8 for _ in range(5)]
    for j in range(8):
        x0, x1, x2, x3 = x[j], x[8 + j], x[16 + j], x[24 + j]
        d, e = (x1 - x3) * R2, (x1 + x3) * R2
        s02, s13 = x0 + x2, x1 + x3
        a[0][j] = (s02 + s13, None)
        a[4][j] = (s02 - s13, None)
        a[2][j] = (x0 - x2, x3 - x1)
        a[1][j] = (x0 + d, -(x2 + e))
        a[3][j] = (x0 - d, x2 - e)
    out = [None] * 33
    for p in range(5):
        b = [a[p][j] if p * j == 0 else times(a[p][j], -2.0 * math.pi * p * j / 64) for j in range(8)]
        f = fft8(b, -1)
        for q in range(8):
            k = p + 8 * q
            if k <= 32:
                out[k] = f[q]
            elif 1 <= p <= 3:
                out[64 - k] = conj(f[q])
    return out


def join_rows(q):
    y = [None] * 32
    b = []
    for p in range(5):
        v = [q[p + 8 * i] if p + 8 * i <= 32 else conj(q[64 - p - 8 * i]) for i in range(8)]
        f = fft8(v, 1)
        b.append([f[j] if p * j == 0 else times(f[j], 2.0 * math.pi * p * j / 64) for j in range(8)])
    for j in range(8):
        b0, b4 = b[0][j][0], b[4][j][0]
        even, odd = 0.5 * (b0 + b4), 0.5 * (b0 - b4)
        (r1, i1), (r2, i2), (r3, i3) = b[1][j], b[2][j], b[3][j]
        y[j] = even + r2 + (r1 + r3)
        y[16 + j] = even - r2 + (i3 - i1)
        u, w = R2 * (r1 - r3), R2 * (i1 + i3)
        y[8 + j] = odd - i2 + (u - w)
        y[24 + j] = odd + i2 - (u + w)
    return y


def mixer_kernel(
    key_ref, value_ref, query_ref, up_ref, filt_ref, w_ref,
    cos_ref, sin_ref, wc_ref, ws_ref, wct_ref, wst_ref,
    gq_out, back_out, fg_out, gw_out,
    k_own, v_own, q_own, f_own, mix_t, q_t, mix_all, q_all, up_all, w_all, gg_all, sc_all, scl_all,
    ft, it, tab, part, filt_s, mix_s, iq, conv_own, conv_all, back_own, fg_own, gate, gq_all, gq_in, back_in,
    fg_x, fg_half, fg_z, fg_fin, gw_part, gw_x, gw_mid, gw_z, gw_fin, gw_sum,
    m_send, m_recv, u_send, u_recv, r_send, r_recv, p_send, p_recv, q_send, q_recv,
    w_send, w_recv, v_send, v_recv, s_send, s_recv, c_send, c_recv, b_send, b_recv,
    fx_send, fx_recv, fz_send, fz_recv, fa_send, fa_recv,
    g_send, g_recv, wx_send, wx_recv, wz_send, wz_recv, wa_send, wa_recv, local,
):
    at = place()
    dp, ctx, near, zh, zl, x = (at[k] for k in ("dp", "ctx", "near", "zh", "zl", "x"))
    y, core = at["y"], at["core"]
    nctx, nnear, ndp, nz = NZH * NY * NC, NY * NC, NX * NZL, NZH * NZL
    rows = CH // NX
    depth = up_ref.shape[-1]
    seq = nctx * TOK
    wide, narrow = depth // NX, depth // NX // NZL
    half = TOK // 2

    def ctx_order():
        turns = sorted(range(NZH), key=lambda a: -min(a, NZH - a))
        return [
            lax.rem(zh + a, NZH) * nnear + lax.rem(near + b, nnear)
            for a in turns
            for b in range(nnear)
            if a or b
        ]

    other = lax.rem(zl + 1, NZL) * NX + x
    peers = []
    if NZL > 1:
        peers += [(other, lax.rem(zh + s, NZH) * nnear + near) for s in range(1, NZH)]
    peers += [(dp, to) for to in ctx_order()]
    if NZL > 1:
        peers += [(other, ctx)]
    peers += [(zl * NX + lax.rem(x + s, NX), ctx) for s in range(1, NX)]
    barrier = pltpu.get_barrier_semaphore()
    for d, c in peers:
        pl.semaphore_signal(barrier, inc=1, device_id=(d, c), device_id_type=MESH)
    loads = [
        pltpu.make_async_copy(key_ref, k_own, local.at[0]),
        pltpu.make_async_copy(value_ref, v_own, local.at[1]),
        pltpu.make_async_copy(query_ref, q_own, local.at[2]),
        pltpu.make_async_copy(filt_ref, f_own, local.at[3]),
        pltpu.make_async_copy(up_ref, up_all.at[near], local.at[4]),
        pltpu.make_async_copy(w_ref, w_all.at[zh], local.at[5]),
    ]
    for copy in loads:
        copy.start()
    loads[0].wait()
    loads[1].wait()

    def mix_block(j, carry):
        cols = pl.ds(pl.multiple_of(j * 2 * CH, 2 * CH), 2 * CH)
        mixed = (k_own[:, cols].astype(F32) * v_own[:, cols].astype(F32)).astype(BF)
        turned = mixed.astype(F32).T.astype(BF)
        mix_t[2 * j] = turned[0:CH]
        mix_t[2 * j + 1] = turned[CH : 2 * CH]
        return carry

    lax.fori_loop(0, nctx // 2, mix_block, 0)
    mix_all[ctx] = mix_t[ctx]
    pl.semaphore_wait(barrier, len(peers))

    ms = []
    for s, to in enumerate(ctx_order(), 1):
        ms.append(send(mix_t.at[to], mix_all.at[ctx], m_send.at[0], m_recv.at[0], dp, to))
        ms[-1].start()

    mine = pl.ds(pl.multiple_of(x * rows, rows), rows)
    ws = []
    for s in range(1, NZH):
        there = lax.rem(zh + s, NZH) * nnear + near
        ws.append(send(w_ref.at[mine], w_all.at[zh, mine], w_send.at[0], w_recv.at[s], dp, there))
        ws[-1].start()

    def along_y(step):
        return zh * nnear + lax.rem(y + step + NY, NY) * NC + core

    def slot_of(step, dc):
        return lax.rem(y + step + NY, NY) * NC + lax.rem(core + dc, NC)

    partner = zh * nnear + y * NC + lax.rem(core + 1, NC)
    steps = {4: (1, -1), 2: (1,), 1: ()}[NY]
    us = {}
    for order in range(2):
        for step in steps:
            h = order if step > 0 else 1 - order
            piece = pl.ds(h * half, half)
            i = (0 if step > 0 else 1) * 2 + h
            us[step, h] = send(
                up_ref.at[piece], up_all.at[near, piece], u_send.at[0], u_recv.at[i], dp, along_y(step)
            )
            us[step, h].start()
    pair = send(up_ref, up_all.at[near], p_send.at[0], p_recv.at[0], dp, partner)
    pair.start()

    loads[2].wait()

    def query_block(j, carry):
        cols = pl.ds(pl.multiple_of(j * 2 * CH, 2 * CH), 2 * CH)
        turned = q_own[:, cols].astype(F32).T.astype(BF)
        first = 2 * j
        q_t[lax.rem(first, nnear), first // nnear] = turned[0:CH]
        q_t[lax.rem(first + 1, nnear), (first + 1) // nnear] = turned[CH : 2 * CH]
        return carry

    lax.fori_loop(0, nctx // 2, query_block, 0)
    qs = {}
    for dy in sorted(range(NY), key=lambda a: min(a, NY - a)):
        for dc in range(NC):
            if dy or dc:
                to = slot_of(dy, dc)
                s = dy * NC + dc
                qs[dy, dc] = send(
                    q_t.at[to], q_all.at[near], q_send.at[0], q_recv.at[s], dp, zh * nnear + to
                )
                qs[dy, dc].start()
    q_all[near] = q_t[near]

    scale = 2.0 / 8192
    tab[0] = cos_ref[...]
    tab[1] = -sin_ref[...]
    tab[2] = cos_ref[...] * scale
    tab[3] = sin_ref[...] * scale

    def build(k, carry):
        a, b = tab[0], tab[1]
        ft[k, 0:128, 0:128] = a.astype(BF)
        ft[k, 128:256, 128:256] = a.astype(BF)
        ft[k, 0:128, 128:256] = b.astype(BF)
        ft[k, 128:256, 0:128] = (-b).astype(BF)
        c, s = wc_ref[...], ws_ref[...]
        tab[0] = a * c + b * s
        tab[1] = b * c - a * s
        a, b = tab[2], tab[3]
        it[k, 0:128, 0:128] = a.astype(BF)
        it[k, 128:256, 128:256] = a.astype(BF)
        it[k, 0:128, 128:256] = b.astype(BF)
        it[k, 128:256, 0:128] = (-b).astype(BF)
        c, s = wct_ref[...], wst_ref[...]
        tab[2] = a * c - b * s
        tab[3] = b * c + a * s
        return carry

    lax.fori_loop(0, 33, build, 0)

    def sections(source, lo_block=0, blocks=CH // 16):
        def body(block, carry):
            at16 = pl.ds(pl.multiple_of(block * 16, 16), 16)
            for lo in (0, 8):
                to = pl.ds(pl.multiple_of(block * 16 + lo, 8), 8)
                if source is None:
                    v = [f_own[to, n * TOK : (n + 1) * TOK] for n in range(nctx)]
                else:
                    v = [source[n, at16].astype(F32)[lo : lo + 8] for n in range(nctx)]
                v += [jnp.zeros_like(v[0])] * (32 - nctx)
                for k, (re, im) in enumerate(split_rows(v)):
                    part[k, to, 0:128] = re
                    part[k, to, 128:256] = jnp.zeros_like(re) if im is None else im
            return carry

        lax.fori_loop(lo_block, lo_block + blocks, body, 0)

    def rejoin(lo_row, target, lo_block=0, blocks=CH // 16):
        def body(block, carry):
            at16 = pl.ds(pl.multiple_of(block * 16, 16), 16)
            halves = []
            for lo in (0, 8):
                to = pl.ds(pl.multiple_of(lo_row + block * 16 + lo, 8), 8)
                halves.append(
                    join_rows([(iq[k, to, 0:128], iq[k, to, 128:256]) for k in range(33)])
                )
            for n in range(nctx):
                value = jnp.concatenate([halves[0][n], halves[1][n]], axis=0).astype(BF)
                if target is fg_own:
                    target[at16, n * TOK : (n + 1) * TOK] = value
                else:
                    target[n, at16] = value
            return carry

        lax.fori_loop(lo_block, lo_block + blocks, body, 0)

    def forward(k):
        full = jnp.dot(part[k].astype(BF), ft[k], preferred_element_type=F32)
        return full[:, 0:128], full[:, 128:256]

    loads[3].wait()
    sections(None)

    rs = []
    if NY == 4:
        for step, h in ((1, 0), (-1, 1)):
            us[step, h].wait_recv()
            piece = up_all.at[slot_of(-step, 0), pl.ds(h * half, half)]
            rs.append(send(piece, piece, r_send.at[0], r_recv.at[h], dp, along_y(step)))
            rs[-1].start()

    def filter_step(k, carry):
        re, im = forward(k)
        filt_s[k, :, 0:128] = re
        filt_s[k, :, 128:256] = im
        return carry

    lax.fori_loop(0, 33, filter_step, 0, unroll=UNROLL)

    drain(mix_all.at[pl.ds(0, nctx - 1)], m_recv.at[0])
    sections(mix_all)

    def conv_step(k, carry):
        mr, mi = forward(k)
        mix_s[k, :, 0:128] = mr
        mix_s[k, :, 128:256] = mi
        fr, fi = filt_s[k, :, 0:128], filt_s[k, :, 128:256]
        both = jnp.concatenate([fr * mr - fi * mi, fr * mi + fi * mr], axis=1).astype(BF)
        iq[k, 0:CH] = jnp.dot(both, it[k], preferred_element_type=F32)
        return carry

    lax.fori_loop(0, 33, conv_step, 0, unroll=UNROLL)
    rejoin(0, conv_own)
    cs = []
    for s in range(1, NZH):
        to = lax.rem(zh + s, NZH)
        cs.append(
            send(
                conv_own.at[pl.ds(to * nnear, nnear)], conv_all.at[zh],
                c_send.at[0], c_recv.at[0], dp, to * nnear + near,
            )
        )
        cs[-1].start()
    for i in range(nnear):
        conv_all[zh, i] = conv_own[zh * nnear + i]

    vs = []
    for s, copy in enumerate(ws, 1):
        copy.wait_recv()
        shard = lax.rem(zh + NZH - s, NZH)
        for t in range(1, NX):
            there = zl * NX + lax.rem(x + t, NX)
            piece = w_all.at[shard, mine]
            vs.append(send(piece, piece, v_send.at[0], v_recv.at[0], there, ctx))
            vs[-1].start()
    relays = []

    def relay(slot, index):
        piece = up_all.at[slot]
        relays.append(send(piece, piece, p_send.at[0], p_recv.at[index], dp, partner))
        relays[-1].start()

    for i, step in enumerate(steps):
        for h in range(2):
            if not (NY == 4 and (step, h) in ((1, 0), (-1, 1))):
                us[step, h].wait_recv()
        relay(slot_of(-step, 0), 1 + i)

    far = slot_of(2, 0)
    loads[4].wait()
    loads[5].wait()
    if vs:
        drain(w_all.at[pl.ds(0, NZH - 1), pl.ds(0, CH - rows)], v_recv.at[0])
    ss = [[], []]

    def work(yy, k):
        w = w_all[...].reshape(NZH * CH, depth)
        up = up_all[pl.ds(yy * NC, NC)].reshape(NC * TOK, depth)
        both = lax.dot_general(
            w, up, (((1,), (1,)), ((), ())), preferred_element_type=F32
        ).astype(BF)
        for c in range(NC):
            slot = yy * NC + c
            gg = both[:, c * TOK : (c + 1) * TOK].reshape(NZH, CH, TOK)
            gg_all[slot] = gg
            sc_all[slot] = (gg.astype(F32) * q_all[slot].astype(F32)).astype(BF)
            n = zh * nnear + slot
            for s in range(1, NZH):
                to = lax.rem(zh + s, NZH)
                for g in range(2):
                    group = pl.ds(g * HALF, HALF)
                    ss[g].append(
                        send(
                            sc_all.at[slot, to, group], scl_all.at[n, group],
                            s_send.at[g], s_recv.at[g], dp, to * nnear + near,
                        )
                    )
                ss[0][-1].start()
            scl_all[n] = sc_all[slot, zh]

    def need(dy):
        for dc in range(NC):
            if dy or dc:
                qs[dy, dc].wait_recv()

    need(0)
    pair.wait_recv()
    work(y, 0)
    for i, step in enumerate(steps):
        need(step % NY)
        relays[i].wait_recv()
        work(lax.rem(y - step + NY, NY), 1 + i)
    if NY == 4:
        need(2)
        for copy in rs:
            copy.wait_recv()
        relay(far, 3)
        relays[2].wait_recv()
        work(lax.rem(y + 2, NY), 3)
    for copy in ss[1]:
        copy.start()

    drain(conv_all.at[pl.ds(0, NZH - 1)], c_recv.at[0])
    for i in range(nnear):
        for h in range(NZH):
            conv = conv_all[h, i].astype(F32)
            gq_all[i, h] = (gg_all[i, h].astype(F32) * conv).astype(BF)
            gate[h * CH : (h + 1) * CH, i * TOK : (i + 1) * TOK] = (
                q_all[i, h].astype(F32) * conv
            ).astype(BF)
    wxs = []
    for s in list(range(1, NX)) + [0]:
        to = lax.rem(x + s, NX)
        cols = pl.ds(pl.multiple_of(to * wide, wide), wide)
        up = up_all[:, :, cols].reshape(nnear * TOK, wide)
        gw_part[to] = jnp.dot(gate[...], up, preferred_element_type=F32).astype(BF)
        if s:
            wxs.append(
                send(gw_part.at[to], gw_x.at[x], wx_send.at[0], wx_recv.at[0], zl * NX + to, ctx)
            )
            wxs[-1].start()
    gw_x[x] = gw_part[x]
    gs = []
    for s in range(1, nnear):
        to = lax.rem(near + s, nnear)
        gs.append(
            send(gq_all.at[to], gq_in.at[:, near], g_send.at[0], g_recv.at[0], dp, zh * nnear + to)
        )
        gs[-1].start()
    for h in range(NZH):
        gq_in[h, near] = gq_all[near, h]

    bs, fxs = [[], []], []
    lanes = seq // NX

    def back_group(g):
        group = slice(g * HALF, (g + 1) * HALF)
        group_ds = pl.ds(g * HALF, HALF)

        def back_step(k, carry):
            full = jnp.dot(part[k, group].astype(BF), ft[k], preferred_element_type=F32)
            gr, gi = full[:, 0:128], full[:, 128:256]
            fr, fi = filt_s[k, group, 0:128], filt_s[k, group, 128:256]
            mr, mi = mix_s[k, group, 0:128], mix_s[k, group, 128:256]
            upper = jnp.concatenate([fr * gr + fi * gi, fr * gi - fi * gr], axis=1).astype(BF)
            lower = jnp.concatenate([mr * gr + mi * gi, mr * gi - mi * gr], axis=1).astype(BF)
            both = jnp.concatenate([upper, lower], axis=0)
            out = jnp.dot(both, it[k], preferred_element_type=F32)
            iq[k, group] = out[0:HALF]
            iq[k, CH + g * HALF : CH + (g + 1) * HALF] = out[HALF:CH]
            return carry

        drain(scl_all.at[pl.ds(0, (NZH - 1) * nnear), group_ds], s_recv.at[g])
        sections(scl_all, g * HALF // 16, HALF // 16)
        lax.fori_loop(0, 33, back_step, 0, unroll=UNROLL)
        rejoin(0, back_own, g * HALF // 16, HALF // 16)
        for s, to in enumerate(ctx_order(), 1):
            bs[g].append(
                send(
                    back_own.at[to, group], back_in.at[ctx, group],
                    b_send.at[0], b_recv.at[0], dp, to,
                )
            )
            if g == 0:
                bs[g][-1].start()
        rejoin(CH, fg_own, g * HALF // 16, HALF // 16)
        for s in range(1, NX):
            to = lax.rem(x + s, NX)
            fxs.append(
                send(
                    fg_own.at[group, pl.ds(pl.multiple_of(to * lanes, lanes), lanes)],
                    fg_x.at[x, group],
                    fx_send.at[0], fx_recv.at[0], zl * NX + to, ctx,
                )
            )
            fxs[-1].start()

    back_group(0)
    back_group(1)
    back_in[ctx] = back_own[ctx]
    fg_x[x] = fg_own[:, pl.ds(pl.multiple_of(x * lanes, lanes), lanes)]
    if NX > 1:
        drain(gw_x.at[pl.ds(0, NX - 1)], wx_recv.at[0])
    for h in range(NZH):
        total = gw_x[0, h * CH : (h + 1) * CH].astype(F32)
        for i in range(1, NX):
            total = total + gw_x[i, h * CH : (h + 1) * CH].astype(F32)
        for i in range(NZL):
            gw_mid[h, i] = total[:, i * narrow : (i + 1) * narrow].astype(BF)
    zs = []
    for s in range(NZH):
        for l in range(NZL):
            if s or l:
                to, tl = lax.rem(zh + s, NZH), lax.rem(zl + l, NZL)
                k = s * NZL + l
                zs.append(
                    send(
                        gw_mid.at[to, tl], gw_z.at[zh * NZL + zl],
                        wz_send.at[0], wz_recv.at[0], tl * NX + x, to * nnear + near,
                    )
                )
                zs[-1].start()
    gw_z[zh * NZL + zl] = gw_mid[zh, zl]

    if NX > 1:
        drain(fg_x.at[pl.ds(0, NX - 1)], fx_recv.at[0])
    total = fg_x[0].astype(F32)
    for i in range(1, NX):
        total = total + fg_x[i].astype(F32)
    fg_half[...] = total.astype(BF)
    fzs = []
    for s in range(1, NZL):
        to = lax.rem(zl + s, NZL)
        fzs.append(send(fg_half, fg_z.at[zl], fz_send.at[s], fz_recv.at[s], to * NX + x, ctx))
        fzs[-1].start()
    fg_z[zl] = fg_half[...]
    for copy in bs[1]:
        copy.start()

    for copy in fzs:
        copy.wait_recv()
    total = fg_z[0].astype(F32)
    for i in range(1, NZL):
        total = total + fg_z[i].astype(F32)
    fg_fin[...] = total.astype(BF)
    fas = []
    fslot = fg_out.at[:, pl.ds(pl.multiple_of(x * lanes, lanes), lanes)]
    for s in range(1, NX):
        to = zl * NX + lax.rem(x + s, NX)
        fas.append(send(fg_fin, fslot, fa_send.at[0], fa_recv.at[0], to, ctx))
        fas[-1].start()
    own_fa = pltpu.make_async_copy(fg_fin, fslot, local.at[11])
    own_fa.start()

    drain(gw_z.at[pl.ds(0, nz - 1)], wz_recv.at[0])
    total = gw_z[0].astype(F32)
    for i in range(1, nz):
        total = total + gw_z[i].astype(F32)
    gw_fin[...] = total.astype(BF)
    gw_sum[zl] = gw_fin[...]
    was = []
    if NZL > 1:
        pair_w = send(gw_fin, gw_sum.at[zl], wz_send.at[1], wz_recv.at[1], other, ctx)
        pair_w.start()

    def spread(l, k):
        wslot = gw_out.at[:, pl.ds(pl.multiple_of((x * NZL + l) * narrow, narrow), narrow)]
        for s in range(1, NX):
            to = zl * NX + lax.rem(x + s, NX)
            was.append(send(gw_sum.at[l], wslot, wa_send.at[0], wa_recv.at[0], to, ctx))
            was[-1].start()
        own = pltpu.make_async_copy(gw_sum.at[l], wslot, local.at[9 + k])
        own.start()
        return own

    own_wa = [spread(zl, 0)]
    drain(gq_in.at[:, pl.ds(0, nnear - 1)], g_recv.at[0])

    def query_rows(j, carry):
        cols = pl.ds(pl.multiple_of(j * 2 * CH, 2 * CH), 2 * CH)
        first = 2 * j
        h, i = first // nnear, lax.rem(first, nnear)
        block = jnp.concatenate([gq_in[h, i], gq_in[h, i + 1]], axis=0)
        q_own[:, cols] = block.astype(F32).T.astype(BF)
        return carry

    lax.fori_loop(0, nctx // 2, query_rows, 0)
    out_q = pltpu.make_async_copy(q_own, gq_out, local.at[7])
    out_q.start()
    if NZL > 1:
        pair_w.wait_recv()
        own_wa.append(spread(lax.rem(zl + 1, NZL), 1))
    drain(back_in.at[pl.ds(0, nctx - 1)], b_recv.at[0])

    def back_rows(j, carry):
        cols = pl.ds(pl.multiple_of(j * 2 * CH, 2 * CH), 2 * CH)
        block = jnp.concatenate([back_in[2 * j], back_in[2 * j + 1]], axis=0)
        k_own[:, cols] = block.astype(F32).T.astype(BF)
        return carry

    lax.fori_loop(0, nctx // 2, back_rows, 0)
    out_b = pltpu.make_async_copy(k_own, back_out, local.at[8])
    out_b.start()
    for copy in [out_q, out_b, own_fa] + own_wa:
        copy.wait()
    if NZL > 1:
        pair_w.wait_send()
        for copy in fzs:
            copy.wait_send()
    drain(mix_all.at[pl.ds(0, nctx - 1)], m_send.at[0])
    drain(up_all.at[pl.ds(0, 1 + len(steps) + (NY == 4))], p_send.at[0])
    if steps:
        drain(up_all.at[pl.ds(0, len(steps))], u_send.at[0])
    if NY == 4:
        drain(up_all.at[0], r_send.at[0])
    drain(q_all.at[pl.ds(0, nnear - 1)], q_send.at[0])
    drain(w_all.at[pl.ds(0, NZH - 1), pl.ds(0, rows)], w_send.at[0])
    if vs:
        drain(w_all.at[pl.ds(0, NZH - 1), pl.ds(0, CH - rows)], v_send.at[0])
    for g in range(2):
        drain(scl_all.at[pl.ds(0, (NZH - 1) * nnear), pl.ds(0, HALF)], s_send.at[g])
    drain(conv_all.at[pl.ds(0, NZH - 1)], c_send.at[0])
    drain(back_in.at[pl.ds(0, nctx - 1)], b_send.at[0])
    drain(gq_in.at[:, pl.ds(0, nnear - 1)], g_send.at[0])
    drain(gw_z.at[pl.ds(0, nz - 1)], wz_send.at[0])
    if NX > 1:
        drain(fg_x.at[pl.ds(0, NX - 1)], fx_send.at[0])
        drain(gw_x.at[pl.ds(0, NX - 1)], wx_send.at[0])
        drain(fg_x.at[pl.ds(0, NX - 1)], fa_send.at[0])
        gw_bytes = gw_x.at[pl.ds(0, NX - 1), pl.ds(0, CH), pl.ds(0, NZL * narrow)]
        drain(gw_bytes, wa_send.at[0])
        drain(gw_bytes, wa_recv.at[0])
        drain(fg_x.at[pl.ds(0, NX - 1)], fa_recv.at[0])


def mixer_call(keys, values, queries, up, filters, w):
    nctx, nnear, ndp, nz = NZH * NY * NC, NY * NC, NX * NZL, NZH * NZL
    depth = up.shape[-1]
    seq = nctx * TOK
    wide, narrow = depth // NX, depth // NX // NZL
    rows = CH // NX
    i = np.arange(128)
    angle = 2.0 * np.pi * ((i[:, None] * i[None, :]) % 128) / 128
    step = np.broadcast_to((2.0 * np.pi * i / 8192)[:, None], (128, 128))
    tables = [np.cos(angle), np.sin(angle), np.cos(step), np.sin(step), np.cos(step.T), np.sin(step.T)]
    tables = [jnp.asarray(np.ascontiguousarray(t), F32) for t in tables]
    dma = pltpu.SemaphoreType.DMA
    hbm = pl.BlockSpec(memory_space=pl.ANY)
    vmem = pl.BlockSpec(memory_space=pltpu.VMEM)
    near4 = (nnear, NZH, CH, TOK)
    chans = (nctx, CH, TOK)
    spec = (33, CH, 256)
    sems = [
        1, 1, 1, 4, 1, 2, 1, 4, 1, nnear, 1, NZH, 1, 1, 2, 2, 1, 1, 1, 1,
        1, 1, NZL, NZL, 1, 1, 1, 1, 1, 1, 2, 2, 1, 1,
    ]
    return pl.pallas_call(
        mixer_kernel,
        name="mixer",
        out_shape=[
            jax.ShapeDtypeStruct((TOK, nctx * CH), BF),
            jax.ShapeDtypeStruct((TOK, nctx * CH), BF),
            jax.ShapeDtypeStruct((CH, seq), BF),
            jax.ShapeDtypeStruct((CH, depth), BF),
        ],
        in_specs=[hbm] * 6 + [vmem] * 6,
        out_specs=[hbm] * 4,
        scratch_shapes=[
            pltpu.VMEM((TOK, nctx * CH), BF),
            pltpu.VMEM((TOK, nctx * CH), BF),
            pltpu.VMEM((TOK, nctx * CH), BF),
            pltpu.VMEM((CH, seq), F32),
            pltpu.VMEM(chans, BF),
            pltpu.VMEM(near4, BF),
            pltpu.VMEM(chans, BF),
            pltpu.VMEM(near4, BF),
            pltpu.VMEM((nnear, TOK, depth), BF),
            pltpu.VMEM((NZH, CH, depth), BF),
            pltpu.VMEM(near4, BF),
            pltpu.VMEM(near4, BF),
            pltpu.VMEM(chans, BF),
            pltpu.VMEM((33, 256, 256), BF),
            pltpu.VMEM((33, 256, 256), BF),
            pltpu.VMEM((4, 128, 128), F32),
            pltpu.VMEM(spec, F32),
            pltpu.VMEM(spec, F32),
            pltpu.VMEM(spec, F32),
            pltpu.VMEM((33, 2 * CH, 256), F32),
            pltpu.VMEM(chans, BF),
            pltpu.VMEM((NZH, nnear, CH, TOK), BF),
            pltpu.VMEM(chans, BF),
            pltpu.VMEM((CH, seq), BF),
            pltpu.VMEM((NZH * CH, nnear * TOK), BF),
            pltpu.VMEM(near4, BF),
            pltpu.VMEM((NZH, nnear, CH, TOK), BF),
            pltpu.VMEM(chans, BF),
            pltpu.VMEM((NX, CH, seq // NX), BF),
            pltpu.VMEM((CH, seq // NX), BF),
            pltpu.VMEM((NZL, CH, seq // NX), BF),
            pltpu.VMEM((CH, seq // NX), BF),
            pltpu.VMEM((NX, NZH * CH, wide), BF),
            pltpu.VMEM((NX, NZH * CH, wide), BF),
            pltpu.VMEM((NZH, NZL, CH, narrow), BF),
            pltpu.VMEM((nz, CH, narrow), BF),
            pltpu.VMEM((CH, narrow), BF),
            pltpu.VMEM((NZL, CH, narrow), BF),
        ]
        + [dma((n,)) for n in sems]
        + [dma((12,))],
        compiler_params=pltpu.CompilerParams(
            collective_id=0, has_side_effects=True, vmem_limit_bytes=60 << 20
        ),
    )(keys, values, queries, up, filters, w, *tables)


def per_device(queries, keys, values, upstream, filters, out_weight):
    key_rows, value_rows = keys[0], values[0]
    gq, back, fg, gw = mixer_call(
        key_rows, value_rows, queries[0], upstream[0], filters, out_weight
    )
    back_wide = back.astype(F32)
    grad_keys = (back_wide * value_rows.astype(F32)).astype(BF)
    grad_values = (back_wide * key_rows.astype(F32)).astype(BF)
    return (gq[None], grad_keys[None], grad_values[None], fg.astype(F32), gw.astype(F32))


def solution(mesh):
    rows = P("dp", "ctx", None)
    chans = P("ctx", None)
    return jax.shard_map(
        per_device,
        mesh=mesh,
        in_specs=(rows, rows, rows, rows, chans, chans),
        out_specs=(rows, rows, rows, chans, chans),
        check_vma=False,
    )
```

```python
import functools
import math

import jax
import jax.numpy as jnp
import numpy as np
from jax import lax
from jax.experimental import pallas as pl
from jax.experimental.pallas import tpu as pltpu
from jax.sharding import PartitionSpec as P

NX, NZL, NZH, NY, NC = 4, 2, 4, 4, 2
TOK, CH = 128, 64
HALF = CH // 2
UNROLL = 11
FINISH_STEPS = 2
BF, F32 = jnp.bfloat16, jnp.float32
MESH = pl.DeviceIdType.MESH


def drain(view, sem):
    pltpu.make_async_copy(view, view, sem).wait()


def place():
    dp = lax.axis_index("dp")
    ctx = lax.axis_index("ctx")
    near = NY * NC
    return dict(
        dp=dp,
        ctx=ctx,
        x=lax.rem(dp, NX),
        zl=dp // NX,
        zh=ctx // near,
        near=lax.rem(ctx, near),
        y=lax.rem(ctx, near) // NC,
        core=lax.rem(ctx, NC),
    )


def send(src, dst, ssem, rsem, dp, ctx):
    return pltpu.make_async_remote_copy(
        src_ref=src,
        dst_ref=dst,
        send_sem=ssem,
        recv_sem=rsem,
        device_id=(dp, ctx),
        device_id_type=MESH,
    )


R2 = math.sqrt(0.5)


def add(a, b):
    return tuple(p if q is None else q if p is None else p + q for p, q in zip(a, b))


def neg(a):
    return tuple(None if p is None else -p for p in a)


def sub(a, b):
    return tuple(
        p if q is None else -q if p is None else p - q for p, q in zip(a, b)
    )


def conj(a):
    return (a[0], None if a[1] is None else -a[1])


def turn(a):
    return (None if a[1] is None else -a[1], a[0])


def unturn(a):
    return (a[1], None if a[0] is None else -a[0])


def times(a, angle):
    c, s = math.cos(angle), math.sin(angle)
    if a[1] is None:
        return (a[0] * c, a[0] * s)
    return (a[0] * c - a[1] * s, a[0] * s + a[1] * c)


def fft4(a, b, c, d, sign):
    s0, s1, s2, s3 = add(a, c), sub(a, c), add(b, d), sub(b, d)
    t3 = turn(s3) if sign > 0 else unturn(s3)
    return [add(s0, s2), add(s1, t3), sub(s0, s2), sub(s1, t3)]


def eighth(a, sign):
    if a[1] is None:
        return (a[0] * R2, a[0] * (R2 * sign))
    if sign > 0:
        return ((a[0] - a[1]) * R2, (a[0] + a[1]) * R2)
    return ((a[0] + a[1]) * R2, (a[1] - a[0]) * R2)


def fft8(v, sign):
    even = fft4(v[0], v[2], v[4], v[6], sign)
    odd = fft4(v[1], v[3], v[5], v[7], sign)
    quarter = turn if sign > 0 else unturn
    odd = [odd[0], eighth(odd[1], sign), quarter(odd[2]), quarter(eighth(odd[3], sign))]
    return [add(e, o) for e, o in zip(even, odd)] + [sub(e, o) for e, o in zip(even, odd)]


def split_rows(x):
    a = [[None] * 8 for _ in range(5)]
    for j in range(8):
        x0, x1, x2, x3 = x[j], x[8 + j], x[16 + j], x[24 + j]
        d, e = (x1 - x3) * R2, (x1 + x3) * R2
        s02, s13 = x0 + x2, x1 + x3
        a[0][j] = (s02 + s13, None)
        a[4][j] = (s02 - s13, None)
        a[2][j] = (x0 - x2, x3 - x1)
        a[1][j] = (x0 + d, -(x2 + e))
        a[3][j] = (x0 - d, x2 - e)
    out = [None] * 33
    for p in range(5):
        b = [a[p][j] if p * j == 0 else times(a[p][j], -2.0 * math.pi * p * j / 64) for j in range(8)]
        f = fft8(b, -1)
        for q in range(8):
            k = p + 8 * q
            if k <= 32:
                out[k] = f[q]
            elif 1 <= p <= 3:
                out[64 - k] = conj(f[q])
    return out


def join_rows(q):
    y = [None] * 32
    b = []
    for p in range(5):
        v = [q[p + 8 * i] if p + 8 * i <= 32 else conj(q[64 - p - 8 * i]) for i in range(8)]
        f = fft8(v, 1)
        b.append([f[j] if p * j == 0 else times(f[j], 2.0 * math.pi * p * j / 64) for j in range(8)])
    for j in range(8):
        b0, b4 = b[0][j][0], b[4][j][0]
        even, odd = 0.5 * (b0 + b4), 0.5 * (b0 - b4)
        (r1, i1), (r2, i2), (r3, i3) = b[1][j], b[2][j], b[3][j]
        y[j] = even + r2 + (r1 + r3)
        y[16 + j] = even - r2 + (i3 - i1)
        u, w = R2 * (r1 - r3), R2 * (i1 + i3)
        y[8 + j] = odd - i2 + (u - w)
        y[24 + j] = odd + i2 - (u + w)
    return y


def mixer_kernel(
    key_ref, value_ref, query_ref, up_ref, filt_ref, w_ref,
    table_ref,
    gq_out, back_out, fg_out, gw_out,
    k_own, v_own, q_own, f_own, mix_t, q_t, mix_all, q_all, up_all, w_all, gg_all, sc_all, scl_all,
    ft, it, tab, wave, part, filt_s, mix_s, iq, conv_own, conv_all, back_own, fg_own, gate, gq_all, gq_in, back_in,
    fg_x, fg_half, fg_z, fg_fin, gw_part, gw_x, gw_mid, gw_z, gw_fin, gw_sum,
    m_send, m_recv, u_send, u_recv, r_send, r_recv, p_send, p_recv, q_send, q_recv,
    w_send, w_recv, v_send, v_recv, s_send, s_recv, c_send, c_recv, b_send, b_recv,
    fx_send, fx_recv, fz_send, fz_recv, fa_send, fa_recv,
    g_send, g_recv, wx_send, wx_recv, wz_send, wz_recv, wa_send, wa_recv, local,
):
    at = place()
    dp, ctx, near, zh, zl, x = (at[k] for k in ("dp", "ctx", "near", "zh", "zl", "x"))
    y, core = at["y"], at["core"]
    nctx, nnear, ndp, nz = NZH * NY * NC, NY * NC, NX * NZL, NZH * NZL
    rows = CH // NX
    depth = up_ref.shape[-1]
    seq = nctx * TOK
    wide, narrow = depth // NX, depth // NX // NZL
    half = TOK // 2

    turns = sorted(range(NZH), key=lambda a: -min(a, NZH - a))

    def ctx_order():
        return [
            lax.rem(zh + a, NZH) * nnear + lax.rem(near + b, nnear)
            for a in turns
            for b in range(nnear)
            if a or b
        ]

    other = lax.rem(zl + 1, NZL) * NX + x
    peers = []
    if NZL > 1:
        peers += [(other, lax.rem(zh + s, NZH) * nnear + near) for s in range(1, NZH)]
    peers += [(dp, to) for to in ctx_order()]
    if NZL > 1:
        peers += [(other, ctx)]
    peers += [(zl * NX + lax.rem(x + s, NX), ctx) for s in range(1, NX)]
    barrier = pltpu.get_barrier_semaphore()
    for d, c in peers:
        pl.semaphore_signal(barrier, inc=1, device_id=(d, c), device_id_type=MESH)
    loads = [
        pltpu.make_async_copy(key_ref, k_own, local.at[0]),
        pltpu.make_async_copy(value_ref, v_own, local.at[1]),
        pltpu.make_async_copy(query_ref, q_own, local.at[2]),
        pltpu.make_async_copy(filt_ref, f_own, local.at[3]),
        pltpu.make_async_copy(up_ref, up_all.at[near], local.at[4]),
        pltpu.make_async_copy(w_ref, w_all.at[zh], local.at[5]),
        pltpu.make_async_copy(table_ref, wave, local.at[6]),
    ]
    for copy in loads:
        copy.start()
    loads[0].wait()
    loads[1].wait()

    def mix_block(j, carry):
        cols = pl.ds(pl.multiple_of(j * 2 * CH, 2 * CH), 2 * CH)
        mixed = (k_own[:, cols].astype(F32) * v_own[:, cols].astype(F32)).astype(BF)
        turned = mixed.astype(F32).T.astype(BF)
        mix_t[2 * j] = turned[0:CH]
        mix_t[2 * j + 1] = turned[CH : 2 * CH]
        return carry

    lax.fori_loop(0, nctx // 2, mix_block, 0)
    mix_all[ctx] = mix_t[ctx]
    pl.semaphore_wait(barrier, len(peers))

    def send_mixed(g):
        group = pl.ds(g * HALF, HALF)
        for to in ctx_order():
            send(
                mix_t.at[to, group], mix_all.at[ctx, group], m_send.at[g], m_recv.at[g], dp, to
            ).start()

    send_mixed(0)
    mine = pl.ds(pl.multiple_of(x * rows, rows), rows)
    ws = []
    for s in range(1, NZH):
        there = lax.rem(zh + s, NZH) * nnear + near
        ws.append(send(w_ref.at[mine], w_all.at[zh, mine], w_send.at[0], w_recv.at[s], dp, there))
        ws[-1].start()
    send_mixed(1)

    def along_y(step):
        return zh * nnear + lax.rem(y + step + NY, NY) * NC + core

    def slot_of(step, dc):
        return lax.rem(y + step + NY, NY) * NC + lax.rem(core + dc, NC)

    partner = zh * nnear + y * NC + lax.rem(core + 1, NC)
    steps = {4: (1, -1), 2: (1,), 1: ()}[NY]
    us = {}
    for order in range(2):
        for step in steps:
            h = order if step > 0 else 1 - order
            piece = pl.ds(h * half, half)
            i = (0 if step > 0 else 1) * 2 + h
            us[step, h] = send(
                up_ref.at[piece], up_all.at[near, piece], u_send.at[0], u_recv.at[i], dp, along_y(step)
            )
            us[step, h].start()
    pair = send(up_ref, up_all.at[near], p_send.at[0], p_recv.at[0], dp, partner)
    pair.start()

    loads[2].wait()

    def query_block(j, carry):
        cols = pl.ds(pl.multiple_of(j * 2 * CH, 2 * CH), 2 * CH)
        turned = q_own[:, cols].astype(F32).T.astype(BF)
        first = 2 * j
        q_t[lax.rem(first, nnear), first // nnear] = turned[0:CH]
        q_t[lax.rem(first + 1, nnear), (first + 1) // nnear] = turned[CH : 2 * CH]
        return carry

    lax.fori_loop(0, nctx // 2, query_block, 0)
    qs = {}
    for dy in sorted(range(NY), key=lambda a: min(a, NY - a)):
        for dc in range(NC):
            if dy or dc:
                to = slot_of(dy, dc)
                s = dy * NC + dc
                qs[dy, dc] = send(
                    q_t.at[to], q_all.at[near], q_send.at[0], q_recv.at[s], dp, zh * nnear + to
                )
                qs[dy, dc].start()
    q_all[near] = q_t[near]

    scale = 2.0 / 8192
    loads[6].wait()
    tab[0] = wave[0]
    tab[1] = -wave[1]
    tab[2] = wave[0] * scale
    tab[3] = wave[1] * scale

    def build(k, carry):
        a, b = tab[0], tab[1]
        ft[k, 0:128, 0:128] = a.astype(BF)
        ft[k, 128:256, 128:256] = a.astype(BF)
        ft[k, 0:128, 128:256] = b.astype(BF)
        ft[k, 128:256, 0:128] = (-b).astype(BF)
        c, s = wave[2], wave[3]
        tab[0] = a * c + b * s
        tab[1] = b * c - a * s
        a, b = tab[2], tab[3]
        it[k, 0:128, 0:128] = a.astype(BF)
        it[k, 128:256, 128:256] = a.astype(BF)
        it[k, 0:128, 128:256] = b.astype(BF)
        it[k, 128:256, 0:128] = (-b).astype(BF)
        c, s = wave[4], wave[5]
        tab[2] = a * c - b * s
        tab[3] = b * c + a * s
        return carry

    lax.fori_loop(0, 33, build, 0)

    def sections(source, lo_block=0, blocks=CH // 16):
        def body(block, carry):
            at16 = pl.ds(pl.multiple_of(block * 16, 16), 16)
            for lo in (0, 8):
                to = pl.ds(pl.multiple_of(block * 16 + lo, 8), 8)
                if source is None:
                    v = [f_own[to, n * TOK : (n + 1) * TOK] for n in range(nctx)]
                else:
                    v = [source[n, at16].astype(F32)[lo : lo + 8] for n in range(nctx)]
                v += [jnp.zeros_like(v[0])] * (32 - nctx)
                for k, (re, im) in enumerate(split_rows(v)):
                    part[k, to, 0:128] = re
                    part[k, to, 128:256] = jnp.zeros_like(re) if im is None else im
            return carry

        lax.fori_loop(lo_block, lo_block + blocks, body, 0)

    def rejoin(lo_row, target, lo_block=0, blocks=CH // 16):
        def body(block, carry):
            at16 = pl.ds(pl.multiple_of(block * 16, 16), 16)
            halves = []
            for lo in (0, 8):
                to = pl.ds(pl.multiple_of(lo_row + block * 16 + lo, 8), 8)
                halves.append(
                    join_rows([(iq[k, to, 0:128], iq[k, to, 128:256]) for k in range(33)])
                )
            for n in range(nctx):
                value = jnp.concatenate([halves[0][n], halves[1][n]], axis=0).astype(BF)
                if target is fg_own:
                    target[at16, n * TOK : (n + 1) * TOK] = value
                else:
                    target[n, at16] = value
            return carry

        lax.fori_loop(lo_block, lo_block + blocks, body, 0)

    def forward(k):
        full = jnp.dot(part[k].astype(BF), ft[k], preferred_element_type=F32)
        return full[:, 0:128], full[:, 128:256]

    loads[3].wait()
    sections(None)

    def filter_step(k, carry):
        re, im = forward(k)
        filt_s[k, :, 0:128] = re
        filt_s[k, :, 128:256] = im
        return carry

    lax.fori_loop(0, 33, filter_step, 0, unroll=UNROLL)

    rs = []
    if NY == 4:
        for step, h in ((1, 0), (-1, 1)):
            us[step, h].wait_recv()
            piece = up_all.at[slot_of(-step, 0), pl.ds(h * half, half)]
            rs.append(send(piece, piece, r_send.at[0], r_recv.at[h], dp, along_y(step)))
            rs[-1].start()

    def conv_group(g):
        group = slice(g * HALF, (g + 1) * HALF)
        group_ds = pl.ds(g * HALF, HALF)

        def conv_step(k, carry):
            full = jnp.dot(part[k, group].astype(BF), ft[k], preferred_element_type=F32)
            mr, mi = full[:, 0:128], full[:, 128:256]
            mix_s[k, group, 0:128] = mr
            mix_s[k, group, 128:256] = mi
            fr, fi = filt_s[k, group, 0:128], filt_s[k, group, 128:256]
            both = jnp.concatenate([fr * mr - fi * mi, fr * mi + fi * mr], axis=1).astype(BF)
            iq[k, group] = jnp.dot(both, it[k], preferred_element_type=F32)
            return carry

        drain(mix_all.at[pl.ds(0, nctx - 1), group_ds], m_recv.at[g])
        sections(mix_all, g * HALF // 16, HALF // 16)
        lax.fori_loop(0, 33, conv_step, 0, unroll=UNROLL)
        rejoin(0, conv_own, g * HALF // 16, HALF // 16)
        for s in turns[:-1]:
            to = lax.rem(zh + s, NZH)
            send(
                conv_own.at[pl.ds(to * nnear, nnear), group_ds], conv_all.at[zh, :, group_ds],
                c_send.at[0], c_recv.at[0], dp, to * nnear + near,
            ).start()

    conv_group(0)
    vs = []
    for s, copy in enumerate(ws, 1):
        copy.wait_recv()
        shard = lax.rem(zh + NZH - s, NZH)
        for t in range(1, NX):
            there = zl * NX + lax.rem(x + t, NX)
            piece = w_all.at[shard, mine]
            vs.append(send(piece, piece, v_send.at[0], v_recv.at[0], there, ctx))
            vs[-1].start()
    conv_group(1)
    for i in range(nnear):
        conv_all[zh, i] = conv_own[zh * nnear + i]

    relays = []

    def relay(slot, index):
        piece = up_all.at[slot]
        relays.append(send(piece, piece, p_send.at[0], p_recv.at[index], dp, partner))
        relays[-1].start()

    for i, step in enumerate(steps):
        for h in range(2):
            if not (NY == 4 and (step, h) in ((1, 0), (-1, 1))):
                us[step, h].wait_recv()
        relay(slot_of(-step, 0), 1 + i)
    far = slot_of(2, 0)
    loads[4].wait()
    loads[5].wait()
    if vs:
        drain(w_all.at[pl.ds(0, NZH - 1), pl.ds(0, CH - rows)], v_recv.at[0])
    ss = [[], []]

    def work(yy, k):
        w = w_all[...].reshape(NZH * CH, depth)
        up = up_all[pl.ds(yy * NC, NC)].reshape(NC * TOK, depth)
        both = lax.dot_general(
            w, up, (((1,), (1,)), ((), ())), preferred_element_type=F32
        ).astype(BF)
        for c in range(NC):
            slot = yy * NC + c
            gg = both[:, c * TOK : (c + 1) * TOK].reshape(NZH, CH, TOK)
            gg_all[slot] = gg
            sc_all[slot] = (gg.astype(F32) * q_all[slot].astype(F32)).astype(BF)
            n = zh * nnear + slot
            for s in turns[:-1]:
                to = lax.rem(zh + s, NZH)
                for g in range(2):
                    group = pl.ds(g * HALF, HALF)
                    ss[g].append(
                        send(
                            sc_all.at[slot, to, group], scl_all.at[n, group],
                            s_send.at[g], s_recv.at[g], dp, to * nnear + near,
                        )
                    )
            scl_all[n] = sc_all[slot, zh]

    def need(dy):
        for dc in range(NC):
            if dy or dc:
                qs[dy, dc].wait_recv()

    need(0)
    pair.wait_recv()
    work(y, 0)
    for i, step in enumerate(steps):
        need(step % NY)
        relays[i].wait_recv()
        work(lax.rem(y - step + NY, NY), 1 + i)
    drain(conv_all.at[pl.ds(0, NZH - 1)], c_send.at[0])
    for copy in ss[0]:
        copy.start()
    started = len(ss[0])
    if NY == 4:
        need(2)
        for copy in rs:
            copy.wait_recv()
        relay(far, 3)
        relays[2].wait_recv()
        work(lax.rem(y + 2, NY), 3)
    for copy in ss[0][started:] + ss[1]:
        copy.start()

    drain(conv_all.at[pl.ds(0, NZH - 1)], c_recv.at[0])
    for i in range(nnear):
        for h in range(NZH):
            conv = conv_all[h, i].astype(F32)
            gq_all[i, h] = (gg_all[i, h].astype(F32) * conv).astype(BF)
            gate[h * CH : (h + 1) * CH, i * TOK : (i + 1) * TOK] = (
                q_all[i, h].astype(F32) * conv
            ).astype(BF)
    wxs = []
    for s in list(range(1, NX)) + [0]:
        to = lax.rem(x + s, NX)
        cols = pl.ds(pl.multiple_of(to * wide, wide), wide)
        up = up_all[:, :, cols].reshape(nnear * TOK, wide)
        gw_part[to] = jnp.dot(gate[...], up, preferred_element_type=F32).astype(BF)
        if s:
            wxs.append(
                send(gw_part.at[to], gw_x.at[x], wx_send.at[0], wx_recv.at[0], zl * NX + to, ctx)
            )
            wxs[-1].start()
    gw_x[x] = gw_part[x]
    gs = []
    for s in range(1, nnear):
        to = lax.rem(near + s, nnear)
        gs.append(
            send(gq_all.at[to], gq_in.at[:, near], g_send.at[0], g_recv.at[0], dp, zh * nnear + to)
        )
        gs[-1].start()
    for h in range(NZH):
        gq_in[h, near] = gq_all[near, h]

    bs, fxs = [[], []], []
    lanes = seq // NX

    def back_group(g):
        group = slice(g * HALF, (g + 1) * HALF)
        group_ds = pl.ds(g * HALF, HALF)

        def back_step(k, carry):
            full = jnp.dot(part[k, group].astype(BF), ft[k], preferred_element_type=F32)
            gr, gi = full[:, 0:128], full[:, 128:256]
            fr, fi = filt_s[k, group, 0:128], filt_s[k, group, 128:256]
            mr, mi = mix_s[k, group, 0:128], mix_s[k, group, 128:256]
            upper = jnp.concatenate([fr * gr + fi * gi, fr * gi - fi * gr], axis=1).astype(BF)
            lower = jnp.concatenate([mr * gr + mi * gi, mr * gi - mi * gr], axis=1).astype(BF)
            both = jnp.concatenate([upper, lower], axis=0)
            out = jnp.dot(both, it[k], preferred_element_type=F32)
            iq[k, group] = out[0:HALF]
            iq[k, CH + g * HALF : CH + (g + 1) * HALF] = out[HALF:CH]
            return carry

        drain(scl_all.at[pl.ds(0, (NZH - 1) * nnear), group_ds], s_recv.at[g])
        sections(scl_all, g * HALF // 16, HALF // 16)
        lax.fori_loop(0, 33, back_step, 0, unroll=UNROLL)
        rejoin(CH, fg_own, g * HALF // 16, HALF // 16)
        for s in range(1, NX):
            to = lax.rem(x + s, NX)
            fxs.append(
                send(
                    fg_own.at[group, pl.ds(pl.multiple_of(to * lanes, lanes), lanes)],
                    fg_x.at[x, group],
                    fx_send.at[0], fx_recv.at[0], zl * NX + to, ctx,
                )
            )
            fxs[-1].start()
        rejoin(0, back_own, g * HALF // 16, HALF // 16)
        for s, to in enumerate(ctx_order(), 1):
            bs[g].append(
                send(
                    back_own.at[to, group], back_in.at[ctx, group],
                    b_send.at[0], b_recv.at[0], dp, to,
                )
            )
            if g == 0:
                bs[g][-1].start()

    back_group(0)
    back_group(1)
    back_in[ctx] = back_own[ctx]
    fg_x[x] = fg_own[:, pl.ds(pl.multiple_of(x * lanes, lanes), lanes)]
    if NX > 1:
        drain(gw_x.at[pl.ds(0, NX - 1)], wx_recv.at[0])
    for h in range(NZH):
        total = gw_x[0, h * CH : (h + 1) * CH].astype(F32)
        for i in range(1, NX):
            total = total + gw_x[i, h * CH : (h + 1) * CH].astype(F32)
        for i in range(NZL):
            gw_mid[h, i] = total[:, i * narrow : (i + 1) * narrow].astype(BF)
    zs = []
    for s in range(NZH):
        for l in range(NZL):
            if s or l:
                to, tl = lax.rem(zh + s, NZH), lax.rem(zl + l, NZL)
                k = s * NZL + l
                zs.append(
                    send(
                        gw_mid.at[to, tl], gw_z.at[zh * NZL + zl],
                        wz_send.at[0], wz_recv.at[0], tl * NX + x, to * nnear + near,
                    )
                )
                zs[-1].start()
    gw_z[zh * NZL + zl] = gw_mid[zh, zl]

    if NX > 1:
        drain(fg_x.at[pl.ds(0, NX - 1)], fx_recv.at[0])
    total = fg_x[0].astype(F32)
    for i in range(1, NX):
        total = total + fg_x[i].astype(F32)
    fg_half[...] = total.astype(BF)
    fzs = []
    for s in range(1, NZL):
        to = lax.rem(zl + s, NZL)
        fzs.append(send(fg_half, fg_z.at[zl], fz_send.at[s], fz_recv.at[s], to * NX + x, ctx))
        fzs[-1].start()
    fg_z[zl] = fg_half[...]
    drain(gw_z.at[pl.ds(0, nz - 1)], wz_recv.at[0])
    total = gw_z[0].astype(F32)
    for i in range(1, nz):
        total = total + gw_z[i].astype(F32)
    gw_fin[...] = total.astype(BF)
    gw_sum[zl] = gw_fin[...]
    was = []
    if NZL > 1:
        pair_w = send(gw_fin, gw_sum.at[zl], wz_send.at[1], wz_recv.at[1], other, ctx)
        pair_w.start()

    def spread(l, k):
        wslot = gw_out.at[:, pl.ds(pl.multiple_of((x * NZL + l) * narrow, narrow), narrow)]
        for s in range(1, NX):
            to = zl * NX + lax.rem(x + s, NX)
            was.append(send(gw_sum.at[l], wslot, wa_send.at[0], wa_recv.at[0], to, ctx))
            was[-1].start()
        own = pltpu.make_async_copy(gw_sum.at[l], wslot, local.at[9 + k])
        own.start()
        return own

    for copy in bs[1]:
        copy.start()
    own_wa = [spread(zl, 0)]
    for copy in fzs:
        copy.wait_recv()
    total = fg_z[0].astype(F32)
    for i in range(1, NZL):
        total = total + fg_z[i].astype(F32)
    fg_fin[...] = total.astype(BF)
    fas = []
    fslot = fg_out.at[:, pl.ds(pl.multiple_of(x * lanes, lanes), lanes)]
    for s in range(1, NX):
        to = zl * NX + lax.rem(x + s, NX)
        fas.append(send(fg_fin, fslot, fa_send.at[0], fa_recv.at[0], to, ctx))
        fas[-1].start()
    own_fa = pltpu.make_async_copy(fg_fin, fslot, local.at[11])
    own_fa.start()

    drain(gq_in.at[:, pl.ds(0, nnear - 1)], g_recv.at[0])

    def query_rows(j, carry):
        cols = pl.ds(pl.multiple_of(j * 2 * CH, 2 * CH), 2 * CH)
        first = 2 * j
        h, i = first // nnear, lax.rem(first, nnear)
        block = jnp.concatenate([gq_in[h, i], gq_in[h, i + 1]], axis=0)
        q_own[:, cols] = block.astype(F32).T.astype(BF)
        return carry

    lax.fori_loop(0, nctx // 2, query_rows, 0)
    out_q = pltpu.make_async_copy(q_own, gq_out, local.at[7])
    out_q.start()
    if NZL > 1:
        pair_w.wait_recv()
        own_wa.append(spread(lax.rem(zl + 1, NZL), 1))
    drain(back_in.at[pl.ds(0, nctx - 1)], b_recv.at[0])

    def back_rows(j, carry):
        cols = pl.ds(pl.multiple_of(j * 2 * CH, 2 * CH), 2 * CH)
        block = jnp.concatenate([back_in[2 * j], back_in[2 * j + 1]], axis=0)
        k_own[:, cols] = block.astype(F32).T.astype(BF)
        return carry

    lax.fori_loop(0, nctx // 2, back_rows, 0)
    out_b = pltpu.make_async_copy(k_own, back_out, local.at[8])
    out_b.start()
    for copy in [out_q, out_b, own_fa] + own_wa:
        copy.wait()
    if NZL > 1:
        pair_w.wait_send()
        for copy in fzs:
            copy.wait_send()
    for g in range(2):
        drain(mix_all.at[pl.ds(0, nctx - 1), pl.ds(0, HALF)], m_send.at[g])
    drain(up_all.at[pl.ds(0, 1 + len(steps) + (NY == 4))], p_send.at[0])
    if steps:
        drain(up_all.at[pl.ds(0, len(steps))], u_send.at[0])
    if NY == 4:
        drain(up_all.at[0], r_send.at[0])
    drain(q_all.at[pl.ds(0, nnear - 1)], q_send.at[0])
    drain(w_all.at[pl.ds(0, NZH - 1), pl.ds(0, rows)], w_send.at[0])
    if vs:
        drain(w_all.at[pl.ds(0, NZH - 1), pl.ds(0, CH - rows)], v_send.at[0])
    for g in range(2):
        drain(scl_all.at[pl.ds(0, (NZH - 1) * nnear), pl.ds(0, HALF)], s_send.at[g])
    drain(back_in.at[pl.ds(0, nctx - 1)], b_send.at[0])
    drain(gq_in.at[:, pl.ds(0, nnear - 1)], g_send.at[0])
    drain(gw_z.at[pl.ds(0, nz - 1)], wz_send.at[0])
    if NX > 1:
        drain(fg_x.at[pl.ds(0, NX - 1)], fx_send.at[0])
        drain(gw_x.at[pl.ds(0, NX - 1)], wx_send.at[0])
        drain(fg_x.at[pl.ds(0, NX - 1)], fa_send.at[0])
        gw_bytes = gw_x.at[pl.ds(0, NX - 1), pl.ds(0, CH), pl.ds(0, NZL * narrow)]
        drain(gw_bytes, wa_send.at[0])
        drain(gw_bytes, wa_recv.at[0])
        drain(fg_x.at[pl.ds(0, NX - 1)], fa_recv.at[0])


def mixer_call(keys, values, queries, up, filters, w):
    nctx, nnear, ndp, nz = NZH * NY * NC, NY * NC, NX * NZL, NZH * NZL
    depth = up.shape[-1]
    seq = nctx * TOK
    wide, narrow = depth // NX, depth // NX // NZL
    rows = CH // NX
    i = np.arange(128)
    angle = 2.0 * np.pi * ((i[:, None] * i[None, :]) % 128) / 128
    step = np.broadcast_to((2.0 * np.pi * i / 8192)[:, None], (128, 128))
    tables = [np.cos(angle), np.sin(angle), np.cos(step), np.sin(step), np.cos(step.T), np.sin(step.T)]
    tables = jnp.asarray(np.stack(tables), F32)
    dma = pltpu.SemaphoreType.DMA
    hbm = pl.BlockSpec(memory_space=pl.ANY)
    near4 = (nnear, NZH, CH, TOK)
    chans = (nctx, CH, TOK)
    spec = (33, CH, 256)
    sems = [
        2, 2, 1, 4, 1, 2, 1, 4, 1, nnear, 1, NZH, 1, 1, 2, 2, 1, 1, 1, 1,
        1, 1, NZL, NZL, 1, 1, 1, 1, 1, 1, 2, 2, 1, 1,
    ]
    return pl.pallas_call(
        mixer_kernel,
        name="mixer",
        out_shape=[
            jax.ShapeDtypeStruct((TOK, nctx * CH), BF),
            jax.ShapeDtypeStruct((TOK, nctx * CH), BF),
            jax.ShapeDtypeStruct((CH, seq), BF),
            jax.ShapeDtypeStruct((CH, depth), BF),
        ],
        in_specs=[hbm] * 7,
        out_specs=[hbm] * 4,
        scratch_shapes=[
            pltpu.VMEM((TOK, nctx * CH), BF),
            pltpu.VMEM((TOK, nctx * CH), BF),
            pltpu.VMEM((TOK, nctx * CH), BF),
            pltpu.VMEM((CH, seq), F32),
            pltpu.VMEM(chans, BF),
            pltpu.VMEM(near4, BF),
            pltpu.VMEM(chans, BF),
            pltpu.VMEM(near4, BF),
            pltpu.VMEM((nnear, TOK, depth), BF),
            pltpu.VMEM((NZH, CH, depth), BF),
            pltpu.VMEM(near4, BF),
            pltpu.VMEM(near4, BF),
            pltpu.VMEM(chans, BF),
            pltpu.VMEM((33, 256, 256), BF),
            pltpu.VMEM((33, 256, 256), BF),
            pltpu.VMEM((4, 128, 128), F32),
            pltpu.VMEM((6, 128, 128), F32),
            pltpu.VMEM(spec, F32),
            pltpu.VMEM(spec, F32),
            pltpu.VMEM(spec, F32),
            pltpu.VMEM((33, 2 * CH, 256), F32),
            pltpu.VMEM(chans, BF),
            pltpu.VMEM((NZH, nnear, CH, TOK), BF),
            pltpu.VMEM(chans, BF),
            pltpu.VMEM((CH, seq), BF),
            pltpu.VMEM((NZH * CH, nnear * TOK), BF),
            pltpu.VMEM(near4, BF),
            pltpu.VMEM((NZH, nnear, CH, TOK), BF),
            pltpu.VMEM(chans, BF),
            pltpu.VMEM((NX, CH, seq // NX), BF),
            pltpu.VMEM((CH, seq // NX), BF),
            pltpu.VMEM((NZL, CH, seq // NX), BF),
            pltpu.VMEM((CH, seq // NX), BF),
            pltpu.VMEM((NX, NZH * CH, wide), BF),
            pltpu.VMEM((NX, NZH * CH, wide), BF),
            pltpu.VMEM((NZH, NZL, CH, narrow), BF),
            pltpu.VMEM((nz, CH, narrow), BF),
            pltpu.VMEM((CH, narrow), BF),
            pltpu.VMEM((NZL, CH, narrow), BF),
        ]
        + [dma((n,)) for n in sems]
        + [dma((12,))],
        compiler_params=pltpu.CompilerParams(
            collective_id=0, has_side_effects=True, vmem_limit_bytes=60 << 20
        ),
    )(keys, values, queries, up, filters, w, tables)


def finish_kernel(gq_ref, back_ref, key_ref, value_ref, fg_ref, gw_ref, gq_out, gk_out, gv_out, fg_out, gw_out):
    gq_out[...] = gq_ref[...]
    back = back_ref[...].astype(F32)
    gk_out[...] = (back * value_ref[...].astype(F32)).astype(BF)
    gv_out[...] = (back * key_ref[...].astype(F32)).astype(BF)
    fg_out[...] = fg_ref[...].astype(F32)
    gw_out[...] = gw_ref[...].astype(F32)


def finish_call(gq, back, keys, values, fg, gw):
    steps = FINISH_STEPS
    by_rows = pl.BlockSpec((gq.shape[0] // steps, gq.shape[1]), lambda i: (i, 0))
    by_cols = [pl.BlockSpec((a.shape[0], a.shape[1] // steps), lambda i: (0, i)) for a in (fg, gw)]
    rows = jax.ShapeDtypeStruct(gq.shape, BF)
    return pl.pallas_call(
        finish_kernel,
        name="finish",
        grid=(steps,),
        out_shape=[rows] * 3 + [jax.ShapeDtypeStruct(a.shape, F32) for a in (fg, gw)],
        in_specs=[by_rows] * 4 + by_cols,
        out_specs=[by_rows] * 3 + by_cols,
        compiler_params=pltpu.CompilerParams(vmem_limit_bytes=60 << 20),
    )(gq, back, keys, values, fg, gw)


def per_device(queries, keys, values, upstream, filters, out_weight):
    gq, back, fg, gw = mixer_call(
        keys[0], values[0], queries[0], upstream[0], filters, out_weight
    )
    gq, gk, gv, fg, gw = finish_call(gq, back, keys[0], values[0], fg, gw)
    return gq[None], gk[None], gv[None], fg, gw


def solution(mesh):
    rows = P("dp", "ctx", None)
    chans = P("ctx", None)
    return jax.shard_map(
        per_device,
        mesh=mesh,
        in_specs=(rows, rows, rows, rows, chans, chans),
        out_specs=(rows, rows, rows, chans, chans),
        check_vma=False,
    )
```

```python
import functools
import math

import jax
import jax.numpy as jnp
import numpy as np
from jax import lax
from jax.experimental import pallas as pl
from jax.experimental.pallas import tpu as pltpu
from jax.sharding import PartitionSpec as P

NX, NZL, NZH, NY, NC = 4, 2, 4, 4, 2
TOK, CH = 128, 64
HALF = CH // 2
UNROLL = 11
FINISH_STEPS = 2
BF, F32 = jnp.bfloat16, jnp.float32
MESH = pl.DeviceIdType.MESH


def drain(view, sem):
    pltpu.make_async_copy(view, view, sem).wait()


def place():
    dp = lax.axis_index("dp")
    ctx = lax.axis_index("ctx")
    near = NY * NC
    return dict(
        dp=dp,
        ctx=ctx,
        x=lax.rem(dp, NX),
        zl=dp // NX,
        zh=ctx // near,
        near=lax.rem(ctx, near),
        y=lax.rem(ctx, near) // NC,
        core=lax.rem(ctx, NC),
    )


def send(src, dst, ssem, rsem, dp, ctx):
    return pltpu.make_async_remote_copy(
        src_ref=src,
        dst_ref=dst,
        send_sem=ssem,
        recv_sem=rsem,
        device_id=(dp, ctx),
        device_id_type=MESH,
    )


R2 = math.sqrt(0.5)


def add(a, b):
    return tuple(p if q is None else q if p is None else p + q for p, q in zip(a, b))


def neg(a):
    return tuple(None if p is None else -p for p in a)


def sub(a, b):
    return tuple(
        p if q is None else -q if p is None else p - q for p, q in zip(a, b)
    )


def conj(a):
    return (a[0], None if a[1] is None else -a[1])


def turn(a):
    return (None if a[1] is None else -a[1], a[0])


def unturn(a):
    return (a[1], None if a[0] is None else -a[0])


def times(a, angle):
    c, s = math.cos(angle), math.sin(angle)
    if a[1] is None:
        return (a[0] * c, a[0] * s)
    return (a[0] * c - a[1] * s, a[0] * s + a[1] * c)


def fft4(a, b, c, d, sign):
    s0, s1, s2, s3 = add(a, c), sub(a, c), add(b, d), sub(b, d)
    t3 = turn(s3) if sign > 0 else unturn(s3)
    return [add(s0, s2), add(s1, t3), sub(s0, s2), sub(s1, t3)]


def eighth(a, sign):
    if a[1] is None:
        return (a[0] * R2, a[0] * (R2 * sign))
    if sign > 0:
        return ((a[0] - a[1]) * R2, (a[0] + a[1]) * R2)
    return ((a[0] + a[1]) * R2, (a[1] - a[0]) * R2)


def fft8(v, sign):
    even = fft4(v[0], v[2], v[4], v[6], sign)
    odd = fft4(v[1], v[3], v[5], v[7], sign)
    quarter = turn if sign > 0 else unturn
    odd = [odd[0], eighth(odd[1], sign), quarter(odd[2]), quarter(eighth(odd[3], sign))]
    return [add(e, o) for e, o in zip(even, odd)] + [sub(e, o) for e, o in zip(even, odd)]


def split_rows(x):
    a = [[None] * 8 for _ in range(5)]
    for j in range(8):
        x0, x1, x2, x3 = x[j], x[8 + j], x[16 + j], x[24 + j]
        d, e = (x1 - x3) * R2, (x1 + x3) * R2
        s02, s13 = x0 + x2, x1 + x3
        a[0][j] = (s02 + s13, None)
        a[4][j] = (s02 - s13, None)
        a[2][j] = (x0 - x2, x3 - x1)
        a[1][j] = (x0 + d, -(x2 + e))
        a[3][j] = (x0 - d, x2 - e)
    out = [None] * 33
    for p in range(5):
        b = [a[p][j] if p * j == 0 else times(a[p][j], -2.0 * math.pi * p * j / 64) for j in range(8)]
        f = fft8(b, -1)
        for q in range(8):
            k = p + 8 * q
            if k <= 32:
                out[k] = f[q]
            elif 1 <= p <= 3:
                out[64 - k] = conj(f[q])
    return out


def join_rows(q):
    y = [None] * 32
    b = []
    for p in range(5):
        v = [q[p + 8 * i] if p + 8 * i <= 32 else conj(q[64 - p - 8 * i]) for i in range(8)]
        f = fft8(v, 1)
        b.append([f[j] if p * j == 0 else times(f[j], 2.0 * math.pi * p * j / 64) for j in range(8)])
    for j in range(8):
        b0, b4 = b[0][j][0], b[4][j][0]
        even, odd = 0.5 * (b0 + b4), 0.5 * (b0 - b4)
        (r1, i1), (r2, i2), (r3, i3) = b[1][j], b[2][j], b[3][j]
        y[j] = even + r2 + (r1 + r3)
        y[16 + j] = even - r2 + (i3 - i1)
        u, w = R2 * (r1 - r3), R2 * (i1 + i3)
        y[8 + j] = odd - i2 + (u - w)
        y[24 + j] = odd + i2 - (u + w)
    return y


def mixer_kernel(
    key_ref, value_ref, query_ref, up_ref, filt_ref, w_ref,
    table_ref,
    gq_out, back_out, fg_out, gw_out,
    k_own, v_own, q_own, f_own, mix_t, q_t, mix_all, q_all, up_all, w_all, gg_all, sc_all, scl_all,
    ft, it, tab, wave, part, filt_s, mix_s, iq, conv_own, conv_all, back_own, fg_own, gate, gq_all, gq_in, back_in,
    fg_x, fg_half, fg_z, fg_fin, gw_part, gw_x, gw_mid, gw_z, gw_fin, gw_sum,
    m_send, m_recv, u_send, u_recv, r_send, r_recv, p_send, p_recv, q_send, q_recv,
    w_send, w_recv, v_send, v_recv, s_send, s_recv, c_send, c_recv, b_send, b_recv,
    fx_send, fx_recv, fz_send, fz_recv, fa_send, fa_recv,
    g_send, g_recv, wx_send, wx_recv, wz_send, wz_recv, wa_send, wa_recv, local,
):
    at = place()
    dp, ctx, near, zh, zl, x = (at[k] for k in ("dp", "ctx", "near", "zh", "zl", "x"))
    y, core = at["y"], at["core"]
    nctx, nnear, ndp, nz = NZH * NY * NC, NY * NC, NX * NZL, NZH * NZL
    rows = CH // NX
    depth = up_ref.shape[-1]
    seq = nctx * TOK
    wide, narrow = depth // NX, depth // NX // NZL
    half = TOK // 2

    turns = sorted(range(NZH), key=lambda a: -min(a, NZH - a))

    def ctx_order():
        return [
            lax.rem(zh + a, NZH) * nnear + lax.rem(near + b, nnear)
            for a in turns
            for b in range(nnear)
            if a or b
        ]

    other = lax.rem(zl + 1, NZL) * NX + x
    peers = []
    if NZL > 1:
        peers += [(other, lax.rem(zh + s, NZH) * nnear + near) for s in range(1, NZH)]
    peers += [(dp, to) for to in ctx_order()]
    if NZL > 1:
        peers += [(other, ctx)]
    peers += [(zl * NX + lax.rem(x + s, NX), ctx) for s in range(1, NX)]
    barrier = pltpu.get_barrier_semaphore()
    for d, c in peers:
        pl.semaphore_signal(barrier, inc=1, device_id=(d, c), device_id_type=MESH)
    loads = [
        pltpu.make_async_copy(key_ref, k_own, local.at[0]),
        pltpu.make_async_copy(value_ref, v_own, local.at[1]),
        pltpu.make_async_copy(query_ref, q_own, local.at[2]),
        pltpu.make_async_copy(filt_ref, f_own, local.at[3]),
        pltpu.make_async_copy(up_ref, up_all.at[near], local.at[4]),
        pltpu.make_async_copy(w_ref, w_all.at[zh], local.at[5]),
        pltpu.make_async_copy(table_ref, wave, local.at[6]),
    ]
    for copy in loads:
        copy.start()
    loads[0].wait()
    loads[1].wait()

    def mix_block(j, carry):
        cols = pl.ds(pl.multiple_of(j * 2 * CH, 2 * CH), 2 * CH)
        mixed = (k_own[:, cols].astype(F32) * v_own[:, cols].astype(F32)).astype(BF)
        turned = mixed.astype(F32).T.astype(BF)
        mix_t[2 * j] = turned[0:CH]
        mix_t[2 * j + 1] = turned[CH : 2 * CH]
        return carry

    lax.fori_loop(0, nctx // 2, mix_block, 0, unroll=4)
    mix_all[ctx] = mix_t[ctx]
    pl.semaphore_wait(barrier, len(peers))

    def send_mixed(g):
        group = pl.ds(g * HALF, HALF)
        for to in ctx_order():
            send(
                mix_t.at[to, group], mix_all.at[ctx, group], m_send.at[g], m_recv.at[g], dp, to
            ).start()

    send_mixed(0)
    mine = pl.ds(pl.multiple_of(x * rows, rows), rows)
    ws = []
    for s in range(1, NZH):
        there = lax.rem(zh + s, NZH) * nnear + near
        ws.append(send(w_ref.at[mine], w_all.at[zh, mine], w_send.at[0], w_recv.at[s], dp, there))
        ws[-1].start()
    send_mixed(1)

    def along_y(step):
        return zh * nnear + lax.rem(y + step + NY, NY) * NC + core

    def slot_of(step, dc):
        return lax.rem(y + step + NY, NY) * NC + lax.rem(core + dc, NC)

    partner = zh * nnear + y * NC + lax.rem(core + 1, NC)
    steps = {4: (1, -1), 2: (1,), 1: ()}[NY]
    us = {}
    for order in range(2):
        for step in steps:
            h = order if step > 0 else 1 - order
            piece = pl.ds(h * half, half)
            i = (0 if step > 0 else 1) * 2 + h
            us[step, h] = send(
                up_ref.at[piece], up_all.at[near, piece], u_send.at[0], u_recv.at[i], dp, along_y(step)
            )
            us[step, h].start()
    pair = send(up_ref, up_all.at[near], p_send.at[0], p_recv.at[0], dp, partner)
    pair.start()

    scale = 2.0 / 8192
    loads[6].wait()
    tab[0] = wave[0]
    tab[1] = -wave[1]
    tab[2] = wave[0] * scale
    tab[3] = wave[1] * scale

    def build(k, carry):
        a, b = tab[0], tab[1]
        ft[k, 0:128, 0:128] = a.astype(BF)
        ft[k, 128:256, 128:256] = a.astype(BF)
        ft[k, 0:128, 128:256] = b.astype(BF)
        ft[k, 128:256, 0:128] = (-b).astype(BF)
        c, s = wave[2], wave[3]
        tab[0] = a * c + b * s
        tab[1] = b * c - a * s
        a, b = tab[2], tab[3]
        it[k, 0:128, 0:128] = a.astype(BF)
        it[k, 128:256, 128:256] = a.astype(BF)
        it[k, 0:128, 128:256] = b.astype(BF)
        it[k, 128:256, 0:128] = (-b).astype(BF)
        c, s = wave[4], wave[5]
        tab[2] = a * c - b * s
        tab[3] = b * c + a * s
        return carry

    lax.fori_loop(0, 33, build, 0)

    def sections(source, lo_block=0, blocks=CH // 16):
        def body(block, carry):
            at16 = pl.ds(pl.multiple_of(block * 16, 16), 16)
            for lo in (0, 8):
                to = pl.ds(pl.multiple_of(block * 16 + lo, 8), 8)
                if source is None:
                    v = [f_own[to, n * TOK : (n + 1) * TOK] for n in range(nctx)]
                else:
                    v = [source[n, at16].astype(F32)[lo : lo + 8] for n in range(nctx)]
                v += [jnp.zeros_like(v[0])] * (32 - nctx)
                for k, (re, im) in enumerate(split_rows(v)):
                    part[k, to, 0:128] = re
                    part[k, to, 128:256] = jnp.zeros_like(re) if im is None else im
            return carry

        lax.fori_loop(lo_block, lo_block + blocks, body, 0)

    def rejoin(lo_row, target, lo_block=0, blocks=CH // 16):
        def body(block, carry):
            at16 = pl.ds(pl.multiple_of(block * 16, 16), 16)
            halves = []
            for lo in (0, 8):
                to = pl.ds(pl.multiple_of(lo_row + block * 16 + lo, 8), 8)
                halves.append(
                    join_rows([(iq[k, to, 0:128], iq[k, to, 128:256]) for k in range(33)])
                )
            for n in range(nctx):
                value = jnp.concatenate([halves[0][n], halves[1][n]], axis=0).astype(BF)
                if target is fg_own:
                    target[at16, n * TOK : (n + 1) * TOK] = value
                else:
                    target[n, at16] = value
            return carry

        lax.fori_loop(lo_block, lo_block + blocks, body, 0)

    def forward(k):
        full = jnp.dot(part[k].astype(BF), ft[k], preferred_element_type=F32)
        return full[:, 0:128], full[:, 128:256]

    loads[3].wait()
    sections(None)

    def filter_step(k, carry):
        re, im = forward(k)
        filt_s[k, :, 0:128] = re
        filt_s[k, :, 128:256] = im
        return carry

    lax.fori_loop(0, 33, filter_step, 0, unroll=UNROLL)

    loads[2].wait()

    def query_block(j, carry):
        cols = pl.ds(pl.multiple_of(j * 2 * CH, 2 * CH), 2 * CH)
        turned = q_own[:, cols].astype(F32).T.astype(BF)
        first = 2 * j
        q_t[lax.rem(first, nnear), first // nnear] = turned[0:CH]
        q_t[lax.rem(first + 1, nnear), (first + 1) // nnear] = turned[CH : 2 * CH]
        return carry

    lax.fori_loop(0, nctx // 2, query_block, 0, unroll=4)
    qs = {}
    for dy in sorted(range(NY), key=lambda a: min(a, NY - a)):
        for dc in range(NC):
            if dy or dc:
                to = slot_of(dy, dc)
                s = dy * NC + dc
                qs[dy, dc] = send(
                    q_t.at[to], q_all.at[near], q_send.at[0], q_recv.at[s], dp, zh * nnear + to
                )
                qs[dy, dc].start()
    q_all[near] = q_t[near]

    rs = []
    if NY == 4:
        for step, h in ((1, 0), (-1, 1)):
            us[step, h].wait_recv()
            piece = up_all.at[slot_of(-step, 0), pl.ds(h * half, half)]
            rs.append(send(piece, piece, r_send.at[0], r_recv.at[h], dp, along_y(step)))
            rs[-1].start()

    def conv_group(g):
        group = slice(g * HALF, (g + 1) * HALF)
        group_ds = pl.ds(g * HALF, HALF)

        def conv_step(k, carry):
            full = jnp.dot(part[k, group].astype(BF), ft[k], preferred_element_type=F32)
            mr, mi = full[:, 0:128], full[:, 128:256]
            mix_s[k, group, 0:128] = mr
            mix_s[k, group, 128:256] = mi
            fr, fi = filt_s[k, group, 0:128], filt_s[k, group, 128:256]
            both = jnp.concatenate([fr * mr - fi * mi, fr * mi + fi * mr], axis=1).astype(BF)
            iq[k, group] = jnp.dot(both, it[k], preferred_element_type=F32)
            return carry

        drain(mix_all.at[pl.ds(0, nctx - 1), group_ds], m_recv.at[g])
        sections(mix_all, g * HALF // 16, HALF // 16)
        lax.fori_loop(0, 33, conv_step, 0, unroll=UNROLL)
        rejoin(0, conv_own, g * HALF // 16, HALF // 16)
        for s in turns[:-1]:
            to = lax.rem(zh + s, NZH)
            send(
                conv_own.at[pl.ds(to * nnear, nnear), group_ds], conv_all.at[zh, :, group_ds],
                c_send.at[0], c_recv.at[0], dp, to * nnear + near,
            ).start()

    conv_group(0)
    vs = []
    for s, copy in enumerate(ws, 1):
        copy.wait_recv()
        shard = lax.rem(zh + NZH - s, NZH)
        for t in range(1, NX):
            there = zl * NX + lax.rem(x + t, NX)
            piece = w_all.at[shard, mine]
            vs.append(send(piece, piece, v_send.at[0], v_recv.at[0], there, ctx))
            vs[-1].start()
    conv_group(1)
    for i in range(nnear):
        conv_all[zh, i] = conv_own[zh * nnear + i]

    relays = []

    def relay(slot, index):
        piece = up_all.at[slot]
        relays.append(send(piece, piece, p_send.at[0], p_recv.at[index], dp, partner))
        relays[-1].start()

    for i, step in enumerate(steps):
        for h in range(2):
            if not (NY == 4 and (step, h) in ((1, 0), (-1, 1))):
                us[step, h].wait_recv()
        relay(slot_of(-step, 0), 1 + i)
    far = slot_of(2, 0)
    loads[4].wait()
    loads[5].wait()
    if vs:
        drain(w_all.at[pl.ds(0, NZH - 1), pl.ds(0, CH - rows)], v_recv.at[0])
    ss = [[], []]

    def work(yy, k):
        w = w_all[...].reshape(NZH * CH, depth)
        up = up_all[pl.ds(yy * NC, NC)].reshape(NC * TOK, depth)
        both = lax.dot_general(
            w, up, (((1,), (1,)), ((), ())), preferred_element_type=F32
        ).astype(BF)
        for c in range(NC):
            slot = yy * NC + c
            gg = both[:, c * TOK : (c + 1) * TOK].reshape(NZH, CH, TOK)
            gg_all[slot] = gg
            sc_all[slot] = (gg.astype(F32) * q_all[slot].astype(F32)).astype(BF)
            n = zh * nnear + slot
            for s in turns[:-1]:
                to = lax.rem(zh + s, NZH)
                for g in range(2):
                    group = pl.ds(g * HALF, HALF)
                    ss[g].append(
                        send(
                            sc_all.at[slot, to, group], scl_all.at[n, group],
                            s_send.at[g], s_recv.at[g], dp, to * nnear + near,
                        )
                    )
            scl_all[n] = sc_all[slot, zh]

    def need(dy):
        for dc in range(NC):
            if dy or dc:
                qs[dy, dc].wait_recv()

    need(0)
    pair.wait_recv()
    work(y, 0)
    for i, step in enumerate(steps):
        need(step % NY)
        relays[i].wait_recv()
        work(lax.rem(y - step + NY, NY), 1 + i)
    drain(conv_all.at[pl.ds(0, NZH - 1)], c_send.at[0])
    for copy in ss[0]:
        copy.start()
    started = len(ss[0])
    if NY == 4:
        need(2)
        for copy in rs:
            copy.wait_recv()
        relay(far, 3)
        relays[2].wait_recv()
        work(lax.rem(y + 2, NY), 3)
    for copy in ss[0][started:] + ss[1]:
        copy.start()

    drain(conv_all.at[pl.ds(0, NZH - 1)], c_recv.at[0])
    for i in range(nnear):
        for h in range(NZH):
            conv = conv_all[h, i].astype(F32)
            gq_all[i, h] = (gg_all[i, h].astype(F32) * conv).astype(BF)
            gate[h * CH : (h + 1) * CH, i * TOK : (i + 1) * TOK] = (
                q_all[i, h].astype(F32) * conv
            ).astype(BF)
    wxs = []
    for s in list(range(1, NX)) + [0]:
        to = lax.rem(x + s, NX)
        cols = pl.ds(pl.multiple_of(to * wide, wide), wide)
        up = up_all[:, :, cols].reshape(nnear * TOK, wide)
        gw_part[to] = jnp.dot(gate[...], up, preferred_element_type=F32).astype(BF)
        if s:
            wxs.append(
                send(gw_part.at[to], gw_x.at[x], wx_send.at[0], wx_recv.at[0], zl * NX + to, ctx)
            )
            wxs[-1].start()
    gw_x[x] = gw_part[x]
    gs = []
    for s in range(1, nnear):
        to = lax.rem(near + s, nnear)
        gs.append(
            send(gq_all.at[to], gq_in.at[:, near], g_send.at[0], g_recv.at[0], dp, zh * nnear + to)
        )
        gs[-1].start()
    for h in range(NZH):
        gq_in[h, near] = gq_all[near, h]

    bs, fxs = [[], []], []
    lanes = seq // NX

    def back_group(g):
        group = slice(g * HALF, (g + 1) * HALF)
        group_ds = pl.ds(g * HALF, HALF)

        def back_step(k, carry):
            full = jnp.dot(part[k, group].astype(BF), ft[k], preferred_element_type=F32)
            gr, gi = full[:, 0:128], full[:, 128:256]
            fr, fi = filt_s[k, group, 0:128], filt_s[k, group, 128:256]
            mr, mi = mix_s[k, group, 0:128], mix_s[k, group, 128:256]
            upper = jnp.concatenate([fr * gr + fi * gi, fr * gi - fi * gr], axis=1).astype(BF)
            lower = jnp.concatenate([mr * gr + mi * gi, mr * gi - mi * gr], axis=1).astype(BF)
            both = jnp.concatenate([upper, lower], axis=0)
            out = jnp.dot(both, it[k], preferred_element_type=F32)
            iq[k, group] = out[0:HALF]
            iq[k, CH + g * HALF : CH + (g + 1) * HALF] = out[HALF:CH]
            return carry

        drain(scl_all.at[pl.ds(0, (NZH - 1) * nnear), group_ds], s_recv.at[g])
        sections(scl_all, g * HALF // 16, HALF // 16)
        lax.fori_loop(0, 33, back_step, 0, unroll=UNROLL)
        rejoin(CH, fg_own, g * HALF // 16, HALF // 16)
        for s in range(1, NX):
            to = lax.rem(x + s, NX)
            fxs.append(
                send(
                    fg_own.at[group, pl.ds(pl.multiple_of(to * lanes, lanes), lanes)],
                    fg_x.at[x, group],
                    fx_send.at[0], fx_recv.at[0], zl * NX + to, ctx,
                )
            )
            fxs[-1].start()
        rejoin(0, back_own, g * HALF // 16, HALF // 16)
        for s, to in enumerate(ctx_order(), 1):
            bs[g].append(
                send(
                    back_own.at[to, group], back_in.at[ctx, group],
                    b_send.at[0], b_recv.at[0], dp, to,
                )
            )
            if g == 0 or s > nctx - nnear:
                bs[g][-1].start()

    back_group(0)
    back_group(1)
    back_in[ctx] = back_own[ctx]
    fg_x[x] = fg_own[:, pl.ds(pl.multiple_of(x * lanes, lanes), lanes)]
    if NX > 1:
        drain(gw_x.at[pl.ds(0, NX - 1)], wx_recv.at[0])
    for h in range(NZH):
        total = gw_x[0, h * CH : (h + 1) * CH].astype(F32)
        for i in range(1, NX):
            total = total + gw_x[i, h * CH : (h + 1) * CH].astype(F32)
        for i in range(NZL):
            gw_mid[h, i] = total[:, i * narrow : (i + 1) * narrow].astype(BF)
    zs = []
    for s in range(NZH):
        for l in range(NZL):
            if s or l:
                to, tl = lax.rem(zh + s, NZH), lax.rem(zl + l, NZL)
                k = s * NZL + l
                zs.append(
                    send(
                        gw_mid.at[to, tl], gw_z.at[zh * NZL + zl],
                        wz_send.at[0], wz_recv.at[0], tl * NX + x, to * nnear + near,
                    )
                )
                zs[-1].start()
    gw_z[zh * NZL + zl] = gw_mid[zh, zl]

    if NX > 1:
        drain(fg_x.at[pl.ds(0, NX - 1)], fx_recv.at[0])
    total = fg_x[0].astype(F32)
    for i in range(1, NX):
        total = total + fg_x[i].astype(F32)
    fg_half[...] = total.astype(BF)
    fzs = []
    for s in range(1, NZL):
        to = lax.rem(zl + s, NZL)
        fzs.append(send(fg_half, fg_z.at[zl], fz_send.at[s], fz_recv.at[s], to * NX + x, ctx))
        fzs[-1].start()
    fg_z[zl] = fg_half[...]
    drain(gw_z.at[pl.ds(0, nz - 1)], wz_recv.at[0])
    total = gw_z[0].astype(F32)
    for i in range(1, nz):
        total = total + gw_z[i].astype(F32)
    gw_fin[...] = total.astype(BF)
    gw_sum[zl] = gw_fin[...]
    was = []
    if NZL > 1:
        pair_w = send(gw_fin, gw_sum.at[zl], wz_send.at[1], wz_recv.at[1], other, ctx)
        pair_w.start()

    def spread(l, k):
        wslot = gw_out.at[:, pl.ds(pl.multiple_of((x * NZL + l) * narrow, narrow), narrow)]
        for s in range(1, NX):
            to = zl * NX + lax.rem(x + s, NX)
            was.append(send(gw_sum.at[l], wslot, wa_send.at[0], wa_recv.at[0], to, ctx))
            was[-1].start()
        own = pltpu.make_async_copy(gw_sum.at[l], wslot, local.at[9 + k])
        own.start()
        return own

    for copy in bs[1][: nctx - nnear]:
        copy.start()
    own_wa = [spread(zl, 0)]
    for copy in fzs:
        copy.wait_recv()
    total = fg_z[0].astype(F32)
    for i in range(1, NZL):
        total = total + fg_z[i].astype(F32)
    fg_fin[...] = total.astype(BF)
    fas = []
    fslot = fg_out.at[:, pl.ds(pl.multiple_of(x * lanes, lanes), lanes)]
    for s in range(1, NX):
        to = zl * NX + lax.rem(x + s, NX)
        fas.append(send(fg_fin, fslot, fa_send.at[0], fa_recv.at[0], to, ctx))
        fas[-1].start()
    own_fa = pltpu.make_async_copy(fg_fin, fslot, local.at[11])
    own_fa.start()

    drain(gq_in.at[:, pl.ds(0, nnear - 1)], g_recv.at[0])

    def query_rows(j, carry):
        cols = pl.ds(pl.multiple_of(j * 2 * CH, 2 * CH), 2 * CH)
        first = 2 * j
        h, i = first // nnear, lax.rem(first, nnear)
        block = jnp.concatenate([gq_in[h, i], gq_in[h, i + 1]], axis=0)
        q_own[:, cols] = block.astype(F32).T.astype(BF)
        return carry

    lax.fori_loop(0, nctx // 2, query_rows, 0, unroll=4)
    out_q = pltpu.make_async_copy(q_own, gq_out, local.at[7])
    out_q.start()
    if NZL > 1:
        pair_w.wait_recv()
        own_wa.append(spread(lax.rem(zl + 1, NZL), 1))
    drain(back_in.at[pl.ds(0, nctx - 1)], b_recv.at[0])

    def back_rows(j, carry):
        cols = pl.ds(pl.multiple_of(j * 2 * CH, 2 * CH), 2 * CH)
        block = jnp.concatenate([back_in[2 * j], back_in[2 * j + 1]], axis=0)
        k_own[:, cols] = block.astype(F32).T.astype(BF)
        return carry

    lax.fori_loop(0, nctx // 2, back_rows, 0, unroll=4)
    out_b = pltpu.make_async_copy(k_own, back_out, local.at[8])
    out_b.start()
    for copy in [out_q, out_b, own_fa] + own_wa:
        copy.wait()
    if NZL > 1:
        pair_w.wait_send()
        for copy in fzs:
            copy.wait_send()
    for g in range(2):
        drain(mix_all.at[pl.ds(0, nctx - 1), pl.ds(0, HALF)], m_send.at[g])
    drain(up_all.at[pl.ds(0, 1 + len(steps) + (NY == 4))], p_send.at[0])
    if steps:
        drain(up_all.at[pl.ds(0, len(steps))], u_send.at[0])
    if NY == 4:
        drain(up_all.at[0], r_send.at[0])
    drain(q_all.at[pl.ds(0, nnear - 1)], q_send.at[0])
    drain(w_all.at[pl.ds(0, NZH - 1), pl.ds(0, rows)], w_send.at[0])
    if vs:
        drain(w_all.at[pl.ds(0, NZH - 1), pl.ds(0, CH - rows)], v_send.at[0])
    for g in range(2):
        drain(scl_all.at[pl.ds(0, (NZH - 1) * nnear), pl.ds(0, HALF)], s_send.at[g])
    drain(back_in.at[pl.ds(0, nctx - 1)], b_send.at[0])
    drain(gq_in.at[:, pl.ds(0, nnear - 1)], g_send.at[0])
    drain(gw_z.at[pl.ds(0, nz - 1)], wz_send.at[0])
    if NX > 1:
        drain(fg_x.at[pl.ds(0, NX - 1)], fx_send.at[0])
        drain(gw_x.at[pl.ds(0, NX - 1)], wx_send.at[0])
        drain(fg_x.at[pl.ds(0, NX - 1)], fa_send.at[0])
        gw_bytes = gw_x.at[pl.ds(0, NX - 1), pl.ds(0, CH), pl.ds(0, NZL * narrow)]
        drain(gw_bytes, wa_send.at[0])
        drain(gw_bytes, wa_recv.at[0])
        drain(fg_x.at[pl.ds(0, NX - 1)], fa_recv.at[0])


def mixer_call(keys, values, queries, up, filters, w):
    nctx, nnear, ndp, nz = NZH * NY * NC, NY * NC, NX * NZL, NZH * NZL
    depth = up.shape[-1]
    seq = nctx * TOK
    wide, narrow = depth // NX, depth // NX // NZL
    rows = CH // NX
    i = np.arange(128)
    angle = 2.0 * np.pi * ((i[:, None] * i[None, :]) % 128) / 128
    step = np.broadcast_to((2.0 * np.pi * i / 8192)[:, None], (128, 128))
    tables = [np.cos(angle), np.sin(angle), np.cos(step), np.sin(step), np.cos(step.T), np.sin(step.T)]
    tables = jnp.asarray(np.stack(tables), F32)
    dma = pltpu.SemaphoreType.DMA
    hbm = pl.BlockSpec(memory_space=pl.ANY)
    near4 = (nnear, NZH, CH, TOK)
    chans = (nctx, CH, TOK)
    spec = (33, CH, 256)
    sems = [
        2, 2, 1, 4, 1, 2, 1, 4, 1, nnear, 1, NZH, 1, 1, 2, 2, 1, 1, 1, 1,
        1, 1, NZL, NZL, 1, 1, 1, 1, 1, 1, 2, 2, 1, 1,
    ]
    return pl.pallas_call(
        mixer_kernel,
        name="mixer",
        out_shape=[
            jax.ShapeDtypeStruct((TOK, nctx * CH), BF),
            jax.ShapeDtypeStruct((TOK, nctx * CH), BF),
            jax.ShapeDtypeStruct((CH, seq), BF),
            jax.ShapeDtypeStruct((CH, depth), BF),
        ],
        in_specs=[hbm] * 7,
        out_specs=[hbm] * 4,
        scratch_shapes=[
            pltpu.VMEM((TOK, nctx * CH), BF),
            pltpu.VMEM((TOK, nctx * CH), BF),
            pltpu.VMEM((TOK, nctx * CH), BF),
            pltpu.VMEM((CH, seq), F32),
            pltpu.VMEM(chans, BF),
            pltpu.VMEM(near4, BF),
            pltpu.VMEM(chans, BF),
            pltpu.VMEM(near4, BF),
            pltpu.VMEM((nnear, TOK, depth), BF),
            pltpu.VMEM((NZH, CH, depth), BF),
            pltpu.VMEM(near4, BF),
            pltpu.VMEM(near4, BF),
            pltpu.VMEM(chans, BF),
            pltpu.VMEM((33, 256, 256), BF),
            pltpu.VMEM((33, 256, 256), BF),
            pltpu.VMEM((4, 128, 128), F32),
            pltpu.VMEM((6, 128, 128), F32),
            pltpu.VMEM(spec, F32),
            pltpu.VMEM(spec, F32),
            pltpu.VMEM(spec, F32),
            pltpu.VMEM((33, 2 * CH, 256), F32),
            pltpu.VMEM(chans, BF),
            pltpu.VMEM((NZH, nnear, CH, TOK), BF),
            pltpu.VMEM(chans, BF),
            pltpu.VMEM((CH, seq), BF),
            pltpu.VMEM((NZH * CH, nnear * TOK), BF),
            pltpu.VMEM(near4, BF),
            pltpu.VMEM((NZH, nnear, CH, TOK), BF),
            pltpu.VMEM(chans, BF),
            pltpu.VMEM((NX, CH, seq // NX), BF),
            pltpu.VMEM((CH, seq // NX), BF),
            pltpu.VMEM((NZL, CH, seq // NX), BF),
            pltpu.VMEM((CH, seq // NX), BF),
            pltpu.VMEM((NX, NZH * CH, wide), BF),
            pltpu.VMEM((NX, NZH * CH, wide), BF),
            pltpu.VMEM((NZH, NZL, CH, narrow), BF),
            pltpu.VMEM((nz, CH, narrow), BF),
            pltpu.VMEM((CH, narrow), BF),
            pltpu.VMEM((NZL, CH, narrow), BF),
        ]
        + [dma((n,)) for n in sems]
        + [dma((12,))],
        compiler_params=pltpu.CompilerParams(
            collective_id=0, has_side_effects=True, vmem_limit_bytes=60 << 20
        ),
    )(keys, values, queries, up, filters, w, tables)


def finish_kernel(gq_ref, back_ref, key_ref, value_ref, fg_ref, gw_ref, gq_out, gk_out, gv_out, fg_out, gw_out):
    gq_out[...] = gq_ref[...]
    back = back_ref[...].astype(F32)
    gk_out[...] = (back * value_ref[...].astype(F32)).astype(BF)
    gv_out[...] = (back * key_ref[...].astype(F32)).astype(BF)
    fg_out[...] = fg_ref[...].astype(F32)
    gw_out[...] = gw_ref[...].astype(F32)


def finish_call(gq, back, keys, values, fg, gw):
    steps = FINISH_STEPS
    by_rows = pl.BlockSpec((gq.shape[0] // steps, gq.shape[1]), lambda i: (i, 0))
    by_cols = [pl.BlockSpec((a.shape[0], a.shape[1] // steps), lambda i: (0, i)) for a in (fg, gw)]
    rows = jax.ShapeDtypeStruct(gq.shape, BF)
    return pl.pallas_call(
        finish_kernel,
        name="finish",
        grid=(steps,),
        out_shape=[rows] * 3 + [jax.ShapeDtypeStruct(a.shape, F32) for a in (fg, gw)],
        in_specs=[by_rows] * 4 + by_cols,
        out_specs=[by_rows] * 3 + by_cols,
        compiler_params=pltpu.CompilerParams(vmem_limit_bytes=60 << 20),
    )(gq, back, keys, values, fg, gw)


def per_device(queries, keys, values, upstream, filters, out_weight):
    gq, back, fg, gw = mixer_call(
        keys[0], values[0], queries[0], upstream[0], filters, out_weight
    )
    gq, gk, gv, fg, gw = finish_call(gq, back, keys[0], values[0], fg, gw)
    return gq[None], gk[None], gv[None], fg, gw


def solution(mesh):
    rows = P("dp", "ctx", None)
    chans = P("ctx", None)
    return jax.shard_map(
        per_device,
        mesh=mesh,
        in_specs=(rows, rows, rows, rows, chans, chans),
        out_specs=(rows, rows, rows, chans, chans),
        check_vma=False,
    )
```

```python
import functools
import math

import jax
import jax.numpy as jnp
import numpy as np
from jax import lax
from jax.experimental import pallas as pl
from jax.experimental.pallas import tpu as pltpu
from jax.sharding import PartitionSpec as P

NX, NZL, NZH, NY, NC = 4, 2, 4, 4, 2
TOK, CH = 128, 64
HALF = CH // 2
UNROLL = 11
FINISH_STEPS = 2
BF, F32 = jnp.bfloat16, jnp.float32
MESH = pl.DeviceIdType.MESH


def drain(view, sem):
    pltpu.make_async_copy(view, view, sem).wait()


def place():
    dp = lax.axis_index("dp")
    ctx = lax.axis_index("ctx")
    near = NY * NC
    return dict(
        dp=dp,
        ctx=ctx,
        x=lax.rem(dp, NX),
        zl=dp // NX,
        zh=ctx // near,
        near=lax.rem(ctx, near),
        y=lax.rem(ctx, near) // NC,
        core=lax.rem(ctx, NC),
    )


def send(src, dst, ssem, rsem, dp, ctx):
    return pltpu.make_async_remote_copy(
        src_ref=src,
        dst_ref=dst,
        send_sem=ssem,
        recv_sem=rsem,
        device_id=(dp, ctx),
        device_id_type=MESH,
    )


R2 = math.sqrt(0.5)


def add(a, b):
    return tuple(p if q is None else q if p is None else p + q for p, q in zip(a, b))


def neg(a):
    return tuple(None if p is None else -p for p in a)


def sub(a, b):
    return tuple(
        p if q is None else -q if p is None else p - q for p, q in zip(a, b)
    )


def conj(a):
    return (a[0], None if a[1] is None else -a[1])


def turn(a):
    return (None if a[1] is None else -a[1], a[0])


def unturn(a):
    return (a[1], None if a[0] is None else -a[0])


def times(a, angle):
    c, s = math.cos(angle), math.sin(angle)
    if a[1] is None:
        return (a[0] * c, a[0] * s)
    return (a[0] * c - a[1] * s, a[0] * s + a[1] * c)


def fft4(a, b, c, d, sign):
    s0, s1, s2, s3 = add(a, c), sub(a, c), add(b, d), sub(b, d)
    t3 = turn(s3) if sign > 0 else unturn(s3)
    return [add(s0, s2), add(s1, t3), sub(s0, s2), sub(s1, t3)]


def eighth(a, sign):
    if a[1] is None:
        return (a[0] * R2, a[0] * (R2 * sign))
    if sign > 0:
        return ((a[0] - a[1]) * R2, (a[0] + a[1]) * R2)
    return ((a[0] + a[1]) * R2, (a[1] - a[0]) * R2)


def fft8(v, sign):
    even = fft4(v[0], v[2], v[4], v[6], sign)
    odd = fft4(v[1], v[3], v[5], v[7], sign)
    quarter = turn if sign > 0 else unturn
    odd = [odd[0], eighth(odd[1], sign), quarter(odd[2]), quarter(eighth(odd[3], sign))]
    return [add(e, o) for e, o in zip(even, odd)] + [sub(e, o) for e, o in zip(even, odd)]


def split_rows(x):
    a = [[None] * 8 for _ in range(5)]
    for j in range(8):
        x0, x1, x2, x3 = x[j], x[8 + j], x[16 + j], x[24 + j]
        d, e = (x1 - x3) * R2, (x1 + x3) * R2
        s02, s13 = x0 + x2, x1 + x3
        a[0][j] = (s02 + s13, None)
        a[4][j] = (s02 - s13, None)
        a[2][j] = (x0 - x2, x3 - x1)
        a[1][j] = (x0 + d, -(x2 + e))
        a[3][j] = (x0 - d, x2 - e)
    out = [None] * 33
    for p in range(5):
        b = [a[p][j] if p * j == 0 else times(a[p][j], -2.0 * math.pi * p * j / 64) for j in range(8)]
        f = fft8(b, -1)
        for q in range(8):
            k = p + 8 * q
            if k <= 32:
                out[k] = f[q]
            elif 1 <= p <= 3:
                out[64 - k] = conj(f[q])
    return out


def join_rows(q):
    y = [None] * 32
    b = []
    for p in range(5):
        v = [q[p + 8 * i] if p + 8 * i <= 32 else conj(q[64 - p - 8 * i]) for i in range(8)]
        f = fft8(v, 1)
        b.append([f[j] if p * j == 0 else times(f[j], 2.0 * math.pi * p * j / 64) for j in range(8)])
    for j in range(8):
        b0, b4 = b[0][j][0], b[4][j][0]
        even, odd = 0.5 * (b0 + b4), 0.5 * (b0 - b4)
        (r1, i1), (r2, i2), (r3, i3) = b[1][j], b[2][j], b[3][j]
        y[j] = even + r2 + (r1 + r3)
        y[16 + j] = even - r2 + (i3 - i1)
        u, w = R2 * (r1 - r3), R2 * (i1 + i3)
        y[8 + j] = odd - i2 + (u - w)
        y[24 + j] = odd + i2 - (u + w)
    return y


def mixer_kernel(
    key_ref, value_ref, query_ref, up_ref, filt_ref, w_ref,
    table_ref,
    gq_out, back_out, fg_out, gw_out,
    k_own, v_own, q_own, f_own, mix_t, q_t, mix_all, q_all, up_all, w_all, gg_all, sc_all, scl_all,
    ft, it, tab, wave, part, filt_s, mix_s, iq, conv_own, conv_all, back_own, fg_own, gate, gq_all, gq_in, back_in,
    fg_x, fg_half, fg_z, fg_fin, gw_part, gw_hop, gw_x, gw_mid, gw_z, gw_fin, gw_sum,
    m_send, m_recv, u_send, u_recv, r_send, r_recv, p_send, p_recv, q_send, q_recv,
    w_send, w_recv, v_send, v_recv, s_send, s_recv, c_send, c_recv, b_send, b_recv,
    fx_send, fx_recv, fz_send, fz_recv, fa_send, fa_recv,
    g_send, g_recv, wx_send, wx_recv, hop_recv, wz_send, wz_recv, wa_send, wa_recv, local,
):
    at = place()
    dp, ctx, near, zh, zl, x = (at[k] for k in ("dp", "ctx", "near", "zh", "zl", "x"))
    y, core = at["y"], at["core"]
    nctx, nnear, ndp, nz = NZH * NY * NC, NY * NC, NX * NZL, NZH * NZL
    rows = CH // NX
    depth = up_ref.shape[-1]
    seq = nctx * TOK
    wide, narrow = depth // NX, depth // NX // NZL
    half = TOK // 2

    turns = sorted(range(NZH), key=lambda a: -min(a, NZH - a))

    def ctx_order():
        return [
            lax.rem(zh + a, NZH) * nnear + lax.rem(near + b, nnear)
            for a in turns
            for b in range(nnear)
            if a or b
        ]

    other = lax.rem(zl + 1, NZL) * NX + x
    peers = []
    if NZL > 1:
        peers += [(other, lax.rem(zh + s, NZH) * nnear + near) for s in range(1, NZH)]
    peers += [(dp, to) for to in ctx_order()]
    if NZL > 1:
        peers += [(other, ctx)]
    peers += [(zl * NX + lax.rem(x + s, NX), ctx) for s in range(1, NX)]
    barrier = pltpu.get_barrier_semaphore()
    for d, c in peers:
        pl.semaphore_signal(barrier, inc=1, device_id=(d, c), device_id_type=MESH)
    loads = [
        pltpu.make_async_copy(key_ref, k_own, local.at[0]),
        pltpu.make_async_copy(value_ref, v_own, local.at[1]),
        pltpu.make_async_copy(query_ref, q_own, local.at[2]),
        pltpu.make_async_copy(filt_ref, f_own, local.at[3]),
        pltpu.make_async_copy(up_ref, up_all.at[near], local.at[4]),
        pltpu.make_async_copy(w_ref, w_all.at[zh], local.at[5]),
        pltpu.make_async_copy(table_ref, wave, local.at[6]),
    ]
    for copy in loads:
        copy.start()
    loads[0].wait()
    loads[1].wait()

    def mix_block(j, carry):
        cols = pl.ds(pl.multiple_of(j * 2 * CH, 2 * CH), 2 * CH)
        mixed = (k_own[:, cols].astype(F32) * v_own[:, cols].astype(F32)).astype(BF)
        turned = mixed.astype(F32).T.astype(BF)
        mix_t[2 * j] = turned[0:CH]
        mix_t[2 * j + 1] = turned[CH : 2 * CH]
        return carry

    lax.fori_loop(0, nctx // 2, mix_block, 0, unroll=4)
    mix_all[ctx] = mix_t[ctx]
    pl.semaphore_wait(barrier, len(peers))

    def send_mixed(g):
        group = pl.ds(g * HALF, HALF)
        for to in ctx_order():
            send(
                mix_t.at[to, group], mix_all.at[ctx, group], m_send.at[g], m_recv.at[g], dp, to
            ).start()

    send_mixed(0)
    mine = pl.ds(pl.multiple_of(x * rows, rows), rows)
    ws = []
    for s in range(1, NZH):
        there = lax.rem(zh + s, NZH) * nnear + near
        ws.append(send(w_ref.at[mine], w_all.at[zh, mine], w_send.at[0], w_recv.at[s], dp, there))
        ws[-1].start()
    send_mixed(1)

    def along_y(step):
        return zh * nnear + lax.rem(y + step + NY, NY) * NC + core

    def slot_of(step, dc):
        return lax.rem(y + step + NY, NY) * NC + lax.rem(core + dc, NC)

    partner = zh * nnear + y * NC + lax.rem(core + 1, NC)
    steps = {4: (1, -1), 2: (1,), 1: ()}[NY]
    us = {}
    for order in range(2):
        for step in steps:
            h = order if step > 0 else 1 - order
            piece = pl.ds(h * half, half)
            i = (0 if step > 0 else 1) * 2 + h
            us[step, h] = send(
                up_ref.at[piece], up_all.at[near, piece], u_send.at[0], u_recv.at[i], dp, along_y(step)
            )
            us[step, h].start()
    pair = send(up_ref, up_all.at[near], p_send.at[0], p_recv.at[0], dp, partner)
    pair.start()

    scale = 2.0 / 8192
    loads[6].wait()
    tab[0] = wave[0]
    tab[1] = -wave[1]
    tab[2] = wave[0] * scale
    tab[3] = wave[1] * scale

    def build(k, carry):
        a, b = tab[0], tab[1]
        ft[k, 0:128, 0:128] = a.astype(BF)
        ft[k, 128:256, 128:256] = a.astype(BF)
        ft[k, 0:128, 128:256] = b.astype(BF)
        ft[k, 128:256, 0:128] = (-b).astype(BF)
        c, s = wave[2], wave[3]
        tab[0] = a * c + b * s
        tab[1] = b * c - a * s
        a, b = tab[2], tab[3]
        it[k, 0:128, 0:128] = a.astype(BF)
        it[k, 128:256, 128:256] = a.astype(BF)
        it[k, 0:128, 128:256] = b.astype(BF)
        it[k, 128:256, 0:128] = (-b).astype(BF)
        c, s = wave[4], wave[5]
        tab[2] = a * c - b * s
        tab[3] = b * c + a * s
        return carry

    lax.fori_loop(0, 33, build, 0)

    def sections(source, lo_block=0, blocks=CH // 16):
        def body(block, carry):
            at16 = pl.ds(pl.multiple_of(block * 16, 16), 16)
            for lo in (0, 8):
                to = pl.ds(pl.multiple_of(block * 16 + lo, 8), 8)
                if source is None:
                    v = [f_own[to, n * TOK : (n + 1) * TOK] for n in range(nctx)]
                else:
                    v = [source[n, at16].astype(F32)[lo : lo + 8] for n in range(nctx)]
                v += [jnp.zeros_like(v[0])] * (32 - nctx)
                for k, (re, im) in enumerate(split_rows(v)):
                    part[k, to, 0:128] = re
                    part[k, to, 128:256] = jnp.zeros_like(re) if im is None else im
            return carry

        lax.fori_loop(lo_block, lo_block + blocks, body, 0)

    def rejoin(lo_row, target, lo_block=0, blocks=CH // 16):
        def body(block, carry):
            at16 = pl.ds(pl.multiple_of(block * 16, 16), 16)
            halves = []
            for lo in (0, 8):
                to = pl.ds(pl.multiple_of(lo_row + block * 16 + lo, 8), 8)
                halves.append(
                    join_rows([(iq[k, to, 0:128], iq[k, to, 128:256]) for k in range(33)])
                )
            for n in range(nctx):
                value = jnp.concatenate([halves[0][n], halves[1][n]], axis=0).astype(BF)
                if target is fg_own:
                    target[at16, n * TOK : (n + 1) * TOK] = value
                else:
                    target[n, at16] = value
            return carry

        lax.fori_loop(lo_block, lo_block + blocks, body, 0)

    def forward(k):
        full = jnp.dot(part[k].astype(BF), ft[k], preferred_element_type=F32)
        return full[:, 0:128], full[:, 128:256]

    loads[3].wait()
    sections(None)

    def filter_step(k, carry):
        re, im = forward(k)
        filt_s[k, :, 0:128] = re
        filt_s[k, :, 128:256] = im
        return carry

    lax.fori_loop(0, 33, filter_step, 0, unroll=UNROLL)

    loads[2].wait()

    def query_block(j, carry):
        cols = pl.ds(pl.multiple_of(j * 2 * CH, 2 * CH), 2 * CH)
        turned = q_own[:, cols].astype(F32).T.astype(BF)
        first = 2 * j
        q_t[lax.rem(first, nnear), first // nnear] = turned[0:CH]
        q_t[lax.rem(first + 1, nnear), (first + 1) // nnear] = turned[CH : 2 * CH]
        return carry

    lax.fori_loop(0, nctx // 2, query_block, 0, unroll=4)
    qs = {}
    for dy in sorted(range(NY), key=lambda a: min(a, NY - a)):
        for dc in range(NC):
            if dy or dc:
                to = slot_of(dy, dc)
                s = dy * NC + dc
                qs[dy, dc] = send(
                    q_t.at[to], q_all.at[near], q_send.at[0], q_recv.at[s], dp, zh * nnear + to
                )
                qs[dy, dc].start()
    q_all[near] = q_t[near]

    rs = []
    if NY == 4:
        for step, h in ((1, 0), (-1, 1)):
            us[step, h].wait_recv()
            piece = up_all.at[slot_of(-step, 0), pl.ds(h * half, half)]
            rs.append(send(piece, piece, r_send.at[0], r_recv.at[h], dp, along_y(step)))
            rs[-1].start()

    def conv_group(g):
        group = slice(g * HALF, (g + 1) * HALF)
        group_ds = pl.ds(g * HALF, HALF)

        def conv_step(k, carry):
            full = jnp.dot(part[k, group].astype(BF), ft[k], preferred_element_type=F32)
            mr, mi = full[:, 0:128], full[:, 128:256]
            mix_s[k, group, 0:128] = mr
            mix_s[k, group, 128:256] = mi
            fr, fi = filt_s[k, group, 0:128], filt_s[k, group, 128:256]
            both = jnp.concatenate([fr * mr - fi * mi, fr * mi + fi * mr], axis=1).astype(BF)
            iq[k, group] = jnp.dot(both, it[k], preferred_element_type=F32)
            return carry

        drain(mix_all.at[pl.ds(0, nctx - 1), group_ds], m_recv.at[g])
        sections(mix_all, g * HALF // 16, HALF // 16)
        lax.fori_loop(0, 33, conv_step, 0, unroll=UNROLL)
        rejoin(0, conv_own, g * HALF // 16, HALF // 16)
        for s in turns[:-1]:
            to = lax.rem(zh + s, NZH)
            send(
                conv_own.at[pl.ds(to * nnear, nnear), group_ds], conv_all.at[zh, :, group_ds],
                c_send.at[0], c_recv.at[0], dp, to * nnear + near,
            ).start()

    conv_group(0)
    vs = []
    for s, copy in enumerate(ws, 1):
        copy.wait_recv()
        shard = lax.rem(zh + NZH - s, NZH)
        for t in range(1, NX):
            there = zl * NX + lax.rem(x + t, NX)
            piece = w_all.at[shard, mine]
            vs.append(send(piece, piece, v_send.at[0], v_recv.at[0], there, ctx))
            vs[-1].start()
    conv_group(1)
    for i in range(nnear):
        conv_all[zh, i] = conv_own[zh * nnear + i]

    relays = []

    def relay(slot, index):
        piece = up_all.at[slot]
        relays.append(send(piece, piece, p_send.at[0], p_recv.at[index], dp, partner))
        relays[-1].start()

    for i, step in enumerate(steps):
        for h in range(2):
            if not (NY == 4 and (step, h) in ((1, 0), (-1, 1))):
                us[step, h].wait_recv()
        relay(slot_of(-step, 0), 1 + i)
    far = slot_of(2, 0)
    loads[4].wait()
    loads[5].wait()
    if vs:
        drain(w_all.at[pl.ds(0, NZH - 1), pl.ds(0, CH - rows)], v_recv.at[0])
    ss = [[], []]

    def work(yy, k):
        w = w_all[...].reshape(NZH * CH, depth)
        up = up_all[pl.ds(yy * NC, NC)].reshape(NC * TOK, depth)
        both = lax.dot_general(
            w, up, (((1,), (1,)), ((), ())), preferred_element_type=F32
        ).astype(BF)
        for c in range(NC):
            slot = yy * NC + c
            gg = both[:, c * TOK : (c + 1) * TOK].reshape(NZH, CH, TOK)
            gg_all[slot] = gg
            sc_all[slot] = (gg.astype(F32) * q_all[slot].astype(F32)).astype(BF)
            n = zh * nnear + slot
            for s in turns[:-1]:
                to = lax.rem(zh + s, NZH)
                for g in range(2):
                    group = pl.ds(g * HALF, HALF)
                    ss[g].append(
                        send(
                            sc_all.at[slot, to, group], scl_all.at[n, group],
                            s_send.at[g], s_recv.at[g], dp, to * nnear + near,
                        )
                    )
            scl_all[n] = sc_all[slot, zh]

    def need(dy):
        for dc in range(NC):
            if dy or dc:
                qs[dy, dc].wait_recv()

    need(0)
    pair.wait_recv()
    work(y, 0)
    for i, step in enumerate(steps):
        need(step % NY)
        relays[i].wait_recv()
        work(lax.rem(y - step + NY, NY), 1 + i)
    drain(conv_all.at[pl.ds(0, NZH - 1)], c_send.at[0])
    for copy in ss[0]:
        copy.start()
    started = len(ss[0])
    if NY == 4:
        need(2)
        for copy in rs:
            copy.wait_recv()
        relay(far, 3)
        relays[2].wait_recv()
        work(lax.rem(y + 2, NY), 3)
    for copy in ss[0][started:] + ss[1]:
        copy.start()

    drain(conv_all.at[pl.ds(0, NZH - 1)], c_recv.at[0])
    for i in range(nnear):
        for h in range(NZH):
            conv = conv_all[h, i].astype(F32)
            gq_all[i, h] = (gg_all[i, h].astype(F32) * conv).astype(BF)
            gate[h * CH : (h + 1) * CH, i * TOK : (i + 1) * TOK] = (
                q_all[i, h].astype(F32) * conv
            ).astype(BF)
    crowd = NZH * CH
    low, high = pl.ds(0, crowd // 2), pl.ds(crowd // 2, crowd // 2)
    right, left = lax.rem(x + 1, NX), lax.rem(x + NX - 1, NX)

    def tile(to):
        cols = pl.ds(pl.multiple_of(to * wide, wide), wide)
        up = up_all[:, :, cols].reshape(nnear * TOK, wide)
        gw_part[to] = jnp.dot(gate[...], up, preferred_element_type=F32).astype(BF)

    def pass_on(to, src, dst, hop, i):
        copy = send(src, dst, wx_send.at[0], (hop_recv if hop else wx_recv).at[i], zl * NX + to, ctx)
        copy.start()
        return copy

    far_x = lax.rem(x + 2, NX)
    tile(far_x)
    hops = [
        pass_on(right, gw_part.at[far_x, low], gw_hop.at[0], True, 0),
        pass_on(left, gw_part.at[far_x, high], gw_hop.at[1], True, 1),
    ]
    tile(right)
    pass_on(right, gw_part.at[right, high], gw_x.at[0, high], False, 0)
    tile(left)
    pass_on(left, gw_part.at[left, low], gw_x.at[1, low], False, 0)
    tile(x)
    gs = []
    for s in range(1, nnear):
        to = lax.rem(near + s, nnear)
        gs.append(
            send(gq_all.at[to], gq_in.at[:, near], g_send.at[0], g_recv.at[0], dp, zh * nnear + to)
        )
        gs[-1].start()
    for h in range(NZH):
        gq_in[h, near] = gq_all[near, h]

    hops[0].wait_recv()
    gw_part[right, low] = (gw_part[right, low].astype(F32) + gw_hop[0].astype(F32)).astype(BF)
    pass_on(right, gw_part.at[right, low], gw_x.at[0, low], False, 0)
    hops[1].wait_recv()
    gw_part[left, high] = (gw_part[left, high].astype(F32) + gw_hop[1].astype(F32)).astype(BF)
    pass_on(left, gw_part.at[left, high], gw_x.at[1, high], False, 0)
    bs, fxs = [[], []], []
    lanes = seq // NX

    def back_group(g):
        group = slice(g * HALF, (g + 1) * HALF)
        group_ds = pl.ds(g * HALF, HALF)

        def back_step(k, carry):
            full = jnp.dot(part[k, group].astype(BF), ft[k], preferred_element_type=F32)
            gr, gi = full[:, 0:128], full[:, 128:256]
            fr, fi = filt_s[k, group, 0:128], filt_s[k, group, 128:256]
            mr, mi = mix_s[k, group, 0:128], mix_s[k, group, 128:256]
            upper = jnp.concatenate([fr * gr + fi * gi, fr * gi - fi * gr], axis=1).astype(BF)
            lower = jnp.concatenate([mr * gr + mi * gi, mr * gi - mi * gr], axis=1).astype(BF)
            both = jnp.concatenate([upper, lower], axis=0)
            out = jnp.dot(both, it[k], preferred_element_type=F32)
            iq[k, group] = out[0:HALF]
            iq[k, CH + g * HALF : CH + (g + 1) * HALF] = out[HALF:CH]
            return carry

        drain(scl_all.at[pl.ds(0, (NZH - 1) * nnear), group_ds], s_recv.at[g])
        sections(scl_all, g * HALF // 16, HALF // 16)
        lax.fori_loop(0, 33, back_step, 0, unroll=UNROLL)
        rejoin(CH, fg_own, g * HALF // 16, HALF // 16)
        for s in range(1, NX):
            to = lax.rem(x + s, NX)
            fxs.append(
                send(
                    fg_own.at[group, pl.ds(pl.multiple_of(to * lanes, lanes), lanes)],
                    fg_x.at[x, group],
                    fx_send.at[0], fx_recv.at[0], zl * NX + to, ctx,
                )
            )
            fxs[-1].start()
        rejoin(0, back_own, g * HALF // 16, HALF // 16)
        for s, to in enumerate(ctx_order(), 1):
            bs[g].append(
                send(
                    back_own.at[to, group], back_in.at[ctx, group],
                    b_send.at[0], b_recv.at[0], dp, to,
                )
            )
            if g == 0 or s > nctx - nnear:
                bs[g][-1].start()

    back_group(0)
    back_group(1)
    back_in[ctx] = back_own[ctx]
    fg_x[x] = fg_own[:, pl.ds(pl.multiple_of(x * lanes, lanes), lanes)]
    drain(gw_x, wx_recv.at[0])
    for h in range(NZH):
        band = slice(h * CH, (h + 1) * CH)
        total = gw_part[x, band].astype(F32) + gw_x[0, band].astype(F32) + gw_x[1, band].astype(F32)
        for i in range(NZL):
            gw_mid[h, i] = total[:, i * narrow : (i + 1) * narrow].astype(BF)
    zs = []
    for s in range(NZH):
        for l in range(NZL):
            if s or l:
                to, tl = lax.rem(zh + s, NZH), lax.rem(zl + l, NZL)
                k = s * NZL + l
                zs.append(
                    send(
                        gw_mid.at[to, tl], gw_z.at[zh * NZL + zl],
                        wz_send.at[0], wz_recv.at[0], tl * NX + x, to * nnear + near,
                    )
                )
                zs[-1].start()
    gw_z[zh * NZL + zl] = gw_mid[zh, zl]

    if NX > 1:
        drain(fg_x.at[pl.ds(0, NX - 1)], fx_recv.at[0])
    total = fg_x[0].astype(F32)
    for i in range(1, NX):
        total = total + fg_x[i].astype(F32)
    fg_half[...] = total.astype(BF)
    fzs = []
    for s in range(1, NZL):
        to = lax.rem(zl + s, NZL)
        fzs.append(send(fg_half, fg_z.at[zl], fz_send.at[s], fz_recv.at[s], to * NX + x, ctx))
        fzs[-1].start()
    fg_z[zl] = fg_half[...]
    for copy in bs[1][:nnear]:
        copy.start()
    drain(gw_z.at[pl.ds(0, nz - 1)], wz_recv.at[0])
    total = gw_z[0].astype(F32)
    for i in range(1, nz):
        total = total + gw_z[i].astype(F32)
    gw_fin[...] = total.astype(BF)
    gw_sum[zl] = gw_fin[...]
    was = []
    if NZL > 1:
        pair_w = send(gw_fin, gw_sum.at[zl], wz_send.at[1], wz_recv.at[1], other, ctx)
        pair_w.start()

    def spread(l, k):
        wslot = gw_out.at[:, pl.ds(pl.multiple_of((x * NZL + l) * narrow, narrow), narrow)]
        for s in range(1, NX):
            to = zl * NX + lax.rem(x + s, NX)
            was.append(send(gw_sum.at[l], wslot, wa_send.at[0], wa_recv.at[0], to, ctx))
            was[-1].start()
        own = pltpu.make_async_copy(gw_sum.at[l], wslot, local.at[9 + k])
        own.start()
        return own

    for copy in bs[1][nnear : nctx - nnear]:
        copy.start()
    own_wa = [spread(zl, 0)]
    for copy in fzs:
        copy.wait_recv()
    total = fg_z[0].astype(F32)
    for i in range(1, NZL):
        total = total + fg_z[i].astype(F32)
    fg_fin[...] = total.astype(BF)
    fas = []
    fslot = fg_out.at[:, pl.ds(pl.multiple_of(x * lanes, lanes), lanes)]
    for s in range(1, NX):
        to = zl * NX + lax.rem(x + s, NX)
        fas.append(send(fg_fin, fslot, fa_send.at[0], fa_recv.at[0], to, ctx))
        fas[-1].start()
    own_fa = pltpu.make_async_copy(fg_fin, fslot, local.at[11])
    own_fa.start()

    drain(gq_in.at[:, pl.ds(0, nnear - 1)], g_recv.at[0])

    def query_rows(j, carry):
        cols = pl.ds(pl.multiple_of(j * 2 * CH, 2 * CH), 2 * CH)
        first = 2 * j
        h, i = first // nnear, lax.rem(first, nnear)
        block = jnp.concatenate([gq_in[h, i], gq_in[h, i + 1]], axis=0)
        q_own[:, cols] = block.astype(F32).T.astype(BF)
        return carry

    lax.fori_loop(0, nctx // 2, query_rows, 0, unroll=4)
    out_q = pltpu.make_async_copy(q_own, gq_out, local.at[7])
    out_q.start()
    if NZL > 1:
        pair_w.wait_recv()
        own_wa.append(spread(lax.rem(zl + 1, NZL), 1))
    drain(back_in.at[pl.ds(0, nctx - 1)], b_recv.at[0])

    def back_rows(j, carry):
        cols = pl.ds(pl.multiple_of(j * 2 * CH, 2 * CH), 2 * CH)
        block = jnp.concatenate([back_in[2 * j], back_in[2 * j + 1]], axis=0)
        k_own[:, cols] = block.astype(F32).T.astype(BF)
        return carry

    lax.fori_loop(0, nctx // 2, back_rows, 0, unroll=4)
    out_b = pltpu.make_async_copy(k_own, back_out, local.at[8])
    out_b.start()
    for copy in [out_q, out_b, own_fa] + own_wa:
        copy.wait()
    if NZL > 1:
        pair_w.wait_send()
        for copy in fzs:
            copy.wait_send()
    for g in range(2):
        drain(mix_all.at[pl.ds(0, nctx - 1), pl.ds(0, HALF)], m_send.at[g])
    drain(up_all.at[pl.ds(0, 1 + len(steps) + (NY == 4))], p_send.at[0])
    if steps:
        drain(up_all.at[pl.ds(0, len(steps))], u_send.at[0])
    if NY == 4:
        drain(up_all.at[0], r_send.at[0])
    drain(q_all.at[pl.ds(0, nnear - 1)], q_send.at[0])
    drain(w_all.at[pl.ds(0, NZH - 1), pl.ds(0, rows)], w_send.at[0])
    if vs:
        drain(w_all.at[pl.ds(0, NZH - 1), pl.ds(0, CH - rows)], v_send.at[0])
    for g in range(2):
        drain(scl_all.at[pl.ds(0, (NZH - 1) * nnear), pl.ds(0, HALF)], s_send.at[g])
    drain(back_in.at[pl.ds(0, nctx - 1)], b_send.at[0])
    drain(gq_in.at[:, pl.ds(0, nnear - 1)], g_send.at[0])
    drain(gw_z.at[pl.ds(0, nz - 1)], wz_send.at[0])
    if NX > 1:
        drain(fg_x.at[pl.ds(0, NX - 1)], fx_send.at[0])
        drain(gw_part.at[pl.ds(0, 3)], wx_send.at[0])
        drain(fg_x.at[pl.ds(0, NX - 1)], fa_send.at[0])
        gw_bytes = gw_part.at[pl.ds(0, NX - 1), pl.ds(0, CH), pl.ds(0, NZL * narrow)]
        drain(gw_bytes, wa_send.at[0])
        drain(gw_bytes, wa_recv.at[0])
        drain(fg_x.at[pl.ds(0, NX - 1)], fa_recv.at[0])


def mixer_call(keys, values, queries, up, filters, w):
    nctx, nnear, ndp, nz = NZH * NY * NC, NY * NC, NX * NZL, NZH * NZL
    depth = up.shape[-1]
    seq = nctx * TOK
    wide, narrow = depth // NX, depth // NX // NZL
    rows = CH // NX
    i = np.arange(128)
    angle = 2.0 * np.pi * ((i[:, None] * i[None, :]) % 128) / 128
    step = np.broadcast_to((2.0 * np.pi * i / 8192)[:, None], (128, 128))
    tables = [np.cos(angle), np.sin(angle), np.cos(step), np.sin(step), np.cos(step.T), np.sin(step.T)]
    tables = jnp.asarray(np.stack(tables), F32)
    dma = pltpu.SemaphoreType.DMA
    hbm = pl.BlockSpec(memory_space=pl.ANY)
    near4 = (nnear, NZH, CH, TOK)
    chans = (nctx, CH, TOK)
    spec = (33, CH, 256)
    sems = [
        2, 2, 1, 4, 1, 2, 1, 4, 1, nnear, 1, NZH, 1, 1, 2, 2, 1, 1, 1, 1,
        1, 1, NZL, NZL, 1, 1, 1, 1, 1, 1, 2, 2, 2, 1, 1,
    ]
    return pl.pallas_call(
        mixer_kernel,
        name="mixer",
        out_shape=[
            jax.ShapeDtypeStruct((TOK, nctx * CH), BF),
            jax.ShapeDtypeStruct((TOK, nctx * CH), BF),
            jax.ShapeDtypeStruct((CH, seq), BF),
            jax.ShapeDtypeStruct((CH, depth), BF),
        ],
        in_specs=[hbm] * 7,
        out_specs=[hbm] * 4,
        scratch_shapes=[
            pltpu.VMEM((TOK, nctx * CH), BF),
            pltpu.VMEM((TOK, nctx * CH), BF),
            pltpu.VMEM((TOK, nctx * CH), BF),
            pltpu.VMEM((CH, seq), F32),
            pltpu.VMEM(chans, BF),
            pltpu.VMEM(near4, BF),
            pltpu.VMEM(chans, BF),
            pltpu.VMEM(near4, BF),
            pltpu.VMEM((nnear, TOK, depth), BF),
            pltpu.VMEM((NZH, CH, depth), BF),
            pltpu.VMEM(near4, BF),
            pltpu.VMEM(near4, BF),
            pltpu.VMEM(chans, BF),
            pltpu.VMEM((33, 256, 256), BF),
            pltpu.VMEM((33, 256, 256), BF),
            pltpu.VMEM((4, 128, 128), F32),
            pltpu.VMEM((6, 128, 128), F32),
            pltpu.VMEM(spec, F32),
            pltpu.VMEM(spec, F32),
            pltpu.VMEM(spec, F32),
            pltpu.VMEM((33, 2 * CH, 256), F32),
            pltpu.VMEM(chans, BF),
            pltpu.VMEM((NZH, nnear, CH, TOK), BF),
            pltpu.VMEM(chans, BF),
            pltpu.VMEM((CH, seq), BF),
            pltpu.VMEM((NZH * CH, nnear * TOK), BF),
            pltpu.VMEM(near4, BF),
            pltpu.VMEM((NZH, nnear, CH, TOK), BF),
            pltpu.VMEM(chans, BF),
            pltpu.VMEM((NX, CH, seq // NX), BF),
            pltpu.VMEM((CH, seq // NX), BF),
            pltpu.VMEM((NZL, CH, seq // NX), BF),
            pltpu.VMEM((CH, seq // NX), BF),
            pltpu.VMEM((NX, NZH * CH, wide), BF),
            pltpu.VMEM((2, NZH * CH // 2, wide), BF),
            pltpu.VMEM((2, NZH * CH, wide), BF),
            pltpu.VMEM((NZH, NZL, CH, narrow), BF),
            pltpu.VMEM((nz, CH, narrow), BF),
            pltpu.VMEM((CH, narrow), BF),
            pltpu.VMEM((NZL, CH, narrow), BF),
        ]
        + [dma((n,)) for n in sems]
        + [dma((12,))],
        compiler_params=pltpu.CompilerParams(
            collective_id=0, has_side_effects=True, vmem_limit_bytes=60 << 20
        ),
    )(keys, values, queries, up, filters, w, tables)


def finish_kernel(gq_ref, back_ref, key_ref, value_ref, fg_ref, gw_ref, gq_out, gk_out, gv_out, fg_out, gw_out):
    gq_out[...] = gq_ref[...]
    back = back_ref[...].astype(F32)
    gk_out[...] = (back * value_ref[...].astype(F32)).astype(BF)
    gv_out[...] = (back * key_ref[...].astype(F32)).astype(BF)
    fg_out[...] = fg_ref[...].astype(F32)
    gw_out[...] = gw_ref[...].astype(F32)


def finish_call(gq, back, keys, values, fg, gw):
    steps = FINISH_STEPS
    by_rows = pl.BlockSpec((gq.shape[0] // steps, gq.shape[1]), lambda i: (i, 0))
    by_cols = [pl.BlockSpec((a.shape[0], a.shape[1] // steps), lambda i: (0, i)) for a in (fg, gw)]
    rows = jax.ShapeDtypeStruct(gq.shape, BF)
    return pl.pallas_call(
        finish_kernel,
        name="finish",
        grid=(steps,),
        out_shape=[rows] * 3 + [jax.ShapeDtypeStruct(a.shape, F32) for a in (fg, gw)],
        in_specs=[by_rows] * 4 + by_cols,
        out_specs=[by_rows] * 3 + by_cols,
        compiler_params=pltpu.CompilerParams(vmem_limit_bytes=60 << 20),
    )(gq, back, keys, values, fg, gw)


def per_device(queries, keys, values, upstream, filters, out_weight):
    gq, back, fg, gw = mixer_call(
        keys[0], values[0], queries[0], upstream[0], filters, out_weight
    )
    gq, gk, gv, fg, gw = finish_call(gq, back, keys[0], values[0], fg, gw)
    return gq[None], gk[None], gv[None], fg, gw


def solution(mesh):
    rows = P("dp", "ctx", None)
    chans = P("ctx", None)
    return jax.shard_map(
        per_device,
        mesh=mesh,
        in_specs=(rows, rows, rows, rows, chans, chans),
        out_specs=(rows, rows, rows, chans, chans),
        check_vma=False,
    )
```
